256 devices in a mesh: pos: 32 (over x_lo, z, core), off: 8 (over x_hi, y).
Axes of the slice: x: 4 (x_hi: 2, x_lo: 2; x = x_hi * 2 + x_lo), y: 4, z: 8, core: 2. Of those that a mesh axis runs over, the one named last changes fastest.
Arguments:
- bin_embed: bfloat16 [2048, 128], P('pos'), may hold values from -6 to 6
- block_slot: int32 [32], replicated, may hold values from 0 to 31, each once
- proj_weight: bfloat16 [128, 64], replicated, may hold values from -0.5 to 0.5
- proj_bias: float32 [64], replicated, may hold values from -3 to 3
- conv_weight: bfloat16 [4, 576, 64], replicated, may hold values from -0.25 to 0.25
- conv_bias: float32 [4, 64], replicated, may hold values from -2 to 2
Outputs:
- contact: bfloat16 [32, 8, 64, 4096], P('pos', 'off')
The draws below stay inside these ranges and needn't reach their ends.
Inputs may be any that keep to these rules, and one draw needn't show every extreme that they name: block_slot names every number of 0 to 31 once; bin block b's embeddings are rows block_slot[b] * 64 to block_slot[b] * 64 + 63 of bin_embed.
All inputs are finite; a program needn't handle non-finite values.
Results may differ from the reference program's by a relative error of at most 0.015.
Values may be sent and summed in bfloat16 or wider, within the bound.
A program may use at most 64 MiB of HBM per device.

```python
import jax
import jax.numpy as jnp
import numpy as np
from jax import lax

TILE = 64
CH = 64
EMB = 128
LAYERS = 4
NPOS = 32
NOFF = 8


def shard_levels(rng, dims, shards, low, high):
    def one(dim, shards_of):
        draws = jax.random.uniform(jax.random.fold_in(jax.random.fold_in(rng, 6), dim), (shards_of,), jnp.float32, low / len(shards), high / len(shards))
        return jnp.repeat(jnp.exp(draws), dims[dim] // shards_of).reshape((-1,) + (1,) * (len(dims) - dim - 1))

    factor_of = one(*shards[0])
    for cut in shards[1:]:
        factor_of = factor_of * one(*cut)
    return factor_of


def gaussian(key, dims, width, reach, split=(), kind=jnp.bfloat16):
    drawn = jax.random.normal(key, dims, jnp.float32) * width
    if len(split) > 0:
        drawn = shard_levels(key, dims, split, -0.22, 0.18) * drawn
    return jnp.clip(drawn, min=-reach, max=reach).astype(kind)


def setup_inputs(seed: int = 0) -> dict:
    seeds = jax.random.split(jax.random.key(seed), 7)
    return {
        "bin_embed": gaussian(seeds[0], (NPOS * TILE, EMB), 1.0, 6.0, ((0, 32),)),
        "block_slot": jax.random.permutation(seeds[1], NPOS).astype(jnp.int32),
        "proj_weight": gaussian(seeds[2], (EMB, CH), EMB ** -0.5, 0.5),
        "proj_bias": gaussian(seeds[3], (CH,), 0.5, 3.0, (), jnp.float32),
        "conv_weight": gaussian(seeds[4], (LAYERS, 9 * CH, CH), (9 * CH) ** -0.5, 0.25),
        "conv_bias": gaussian(seeds[5], (LAYERS, CH), 0.3, 2.0, (), jnp.float32),
    }


def flip_tiles(tiles):
    return jnp.swapaxes(tiles, -3, -2)


def reference(bin_embed, block_slot, proj_weight, proj_bias, conv_weight, conv_bias):
    projected = jnp.dot(bin_embed, proj_weight, preferred_element_type=jnp.float32).astype(jnp.bfloat16)
    projected = projected.reshape(NPOS, TILE, CH)[block_slot]
    col_index = (jnp.arange(NPOS)[:, None] + jnp.arange(NOFF)[None, :]) % NPOS
    col_bins = projected[col_index]
    pair_sum = projected[:, None, :, None, :].astype(jnp.float32) + col_bins[:, :, None, :, :].astype(jnp.float32) + proj_bias
    current = pair_sum.astype(jnp.bfloat16)
    for layer_index in range(LAYERS):
        dilation = 2 ** layer_index
        hidden = jax.nn.gelu(current.astype(jnp.float32)).astype(jnp.bfloat16)
        mirrors = []
        for mirror_band in (2, 1):
            if mirror_band < NOFF:
                mirrors.append(jnp.roll(flip_tiles(hidden[:, mirror_band]), mirror_band, axis=0)[:, None])
            else:
                mirrors.append(jnp.zeros_like(hidden[:, :1]))
        beyond = jnp.zeros_like(hidden[:, :1])
        extended = jnp.concatenate(mirrors + [hidden, beyond, beyond], axis=1)
        weights = conv_weight[layer_index].astype(jnp.float32)
        layer_bias = conv_bias[layer_index]

        def one_row(inputs, extended=extended, weights=weights, layer_bias=layer_bias, dilation=dilation):
            position, tile_row = inputs
            rows_out = []
            for shift_row in (-1, 0, 1):
                source = extended[(position + shift_row) % NPOS]
                pieces = [source[np.arange(NOFF) + shift_col - shift_row + 2] for shift_col in (-1, 0, 1)]
                rows_out.append(jnp.concatenate(pieces, axis=2))
            padded = jnp.concatenate(rows_out, axis=1)
            padded = padded[:, TILE - dilation:2 * TILE + dilation, TILE - dilation:2 * TILE + dilation].astype(jnp.float32)
            summed = jnp.zeros((NOFF, TILE, TILE, CH), jnp.float32)
            for row_tap in range(3):
                for col_tap in range(3):
                    tap_index = 3 * row_tap + col_tap
                    window = padded[:, row_tap * dilation:row_tap * dilation + TILE, col_tap * dilation:col_tap * dilation + TILE]
                    summed = summed + jnp.einsum("orcd,de->orce", window, weights[tap_index * CH:(tap_index + 1) * CH])
            return (tile_row.astype(jnp.float32) + summed + layer_bias).astype(jnp.bfloat16)

        current = lax.map(one_row, (jnp.arange(NPOS, dtype=jnp.int32), current))
    return current.reshape(NPOS, NOFF, TILE, TILE * CH)
```

```python
import functools

import jax
import jax.numpy as jnp
from jax import lax
from jax.experimental import pallas as pl
from jax.experimental.pallas import tpu as pltpu
from jax.sharding import PartitionSpec as P

TILE = 64
LAYERS = 4
HALO = 16
SIDE = TILE + 2 * HALO
PAIRS = SIDE // 2
PAD = 8
PITCH = SIDE + 2 * PAD
LANES = 128
F32 = jnp.float32
BF16 = jnp.bfloat16

X_LO, Z, CORE = 2, 8, 2
Z_ORDER = (1, 7, 2, 6, 3, 5, 4)


def low_half(shape):
    return lax.broadcasted_iota(jnp.int32, shape, 1) < LANES // 2


def swap(value):
    return pltpu.roll(value, LANES // 2, 1)


def dup_low(value):
    return jnp.where(low_half(value.shape), value, swap(value))


def dup_high(value):
    return jnp.where(low_half(value.shape), swap(value), value)


def gather_kernel(embed, slots, weight, bias, rows_out, cols_out, bins, cols, z_send, z_recv, x_send, x_recv, c_send, c_recv):
    me = lax.axis_index("pos")
    offset = lax.axis_index("off")
    blocks = X_LO * Z * CORE
    x = me // (Z * CORE)
    z = (me // CORE) % Z
    core = me % CORE

    def index(x_, z_, core_):
        return (x_ * Z + z_) * CORE + core_

    across = index(1 - x, z, core)
    twin = index(x, z, 1 - core)
    barrier = pltpu.get_barrier_semaphore()
    peers = [index(x, (z + step) % Z, core) for step in Z_ORDER] + [across, twin]
    for peer in peers:
        pl.semaphore_signal(barrier, inc=1, device_id={"pos": peer}, device_id_type=pl.DeviceIdType.MESH)
    half = TILE // 2
    packed = [
        jnp.dot(embed[part * half : (part + 1) * half], weight[...], preferred_element_type=F32) for part in range(2)
    ]
    bins[me] = jnp.concatenate(packed, axis=1).astype(BF16)
    pl.semaphore_wait(barrier, len(peers))

    def send(block, peer, send_sem, recv_sem):
        copy = pltpu.make_async_remote_copy(
            src_ref=bins.at[block],
            dst_ref=bins.at[block],
            send_sem=send_sem,
            recv_sem=recv_sem,
            device_id={"pos": peer},
            device_id_type=pl.DeviceIdType.MESH,
        )
        copy.start()
        return copy

    along = {}
    for step in Z_ORDER:
        along[step] = send(me, index(x, (z + step) % Z, core), z_send.at[step], z_recv.at[step])
    sides = {0: send(me, across, x_send.at[0], x_recv.at[0])}
    twins = {0: send(me, twin, c_send.at[0], c_recv.at[0])}
    for step in Z_ORDER:
        along[step].wait_recv()
        block = index(x, (z + Z - step) % Z, core)
        sides[step] = send(block, across, x_send.at[step], x_recv.at[step])
        twins[step] = send(block, twin, c_send.at[step], c_recv.at[step])
    for step in (0,) + Z_ORDER:
        sides[step].wait_recv()
        block = index(1 - x, (z + Z - step) % Z, core)
        twins[Z + step] = send(block, twin, c_send.at[Z + step], c_recv.at[Z + step])
    for step in (0,) + Z_ORDER:
        twins[step].wait_recv()
    for step in (0,) + Z_ORDER:
        twins[Z + step].wait_recv()
    for copy in [*along.values(), *sides.values(), *twins.values()]:
        copy.wait_send()

    def spread(base, out):
        def block(shift):
            return bins[slots[(base + shift + blocks) % blocks]].astype(F32)

        before, here, after = block(-1), block(0), block(1)
        out[0:HALO] = dup_high(before[half - HALO :])
        out[HALO : HALO + half] = dup_low(here)
        out[HALO + half : HALO + TILE] = dup_high(here)
        out[HALO + TILE : SIDE] = dup_low(after[:HALO])

    spread(me, rows_out)
    spread(me + offset, cols)
    even = cols[pl.ds(0, PAIRS, stride=2), :]
    odd = cols[pl.ds(1, PAIRS, stride=2), :]
    bias_twice = jnp.concatenate([bias[...], bias[...]], axis=1)
    cols_out[...] = jnp.where(low_half(even.shape), even, odd) + bias_twice


def gelu(value):
    inner = value * (0.7978845608028654 + 0.035677408136300125 * (value * value))
    half = 0.5 * value
    return half + half * jnp.tanh(inner)


def quads_of(layer):
    if layer == 0:
        return [(j, j + 1) for j in range(1, 47, 2)]
    step = 2 ** (layer - 1)
    low = {1: 2, 2: 4, 3: 8}[layer]
    starts = range(low, PAIRS - low, 2 * step)
    return [(j + k, j + k + step) for j in starts for k in range(step)]


ROWS = {0: (0, 96), 1: (0, 96), 2: (8, 88), 3: (16, 80)}


def at(pair, row):
    return pair * PITCH + PAD + row


def layer_weights(conv, layer, out):
    taps = [conv[layer, tap * TILE : (tap + 1) * TILE, :] for tap in range(9)]
    taps = [jnp.concatenate([tap, tap], axis=1) for tap in taps]
    low = low_half((TILE, LANES))
    zero = jnp.zeros((TILE, LANES), BF16)
    for row_tap in range(3):
        for block in range(8):
            for group in range(2):
                if layer == 0:
                    left = block - 2 - 2 * group + 1
                    right = left - 1
                else:
                    left = right = block // 2 - group
                    if block % 2 == 0:
                        right = -1
                    else:
                        left = -1
                a = taps[3 * row_tap + left] if 0 <= left < 3 else zero
                b = taps[3 * row_tap + right] if 0 <= right < 3 else zero
                value = zero if (a is zero and b is zero) else jnp.where(low, a, b)
                row = (block % 4) * TILE
                out[row_tap * 2 + block // 4, row : row + TILE, group * LANES : (group + 1) * LANES] = value


def swap_pixels(even, odd):
    low = low_half(even.shape)
    return jnp.where(low, even, swap(odd)), jnp.where(low, swap(even), odd)


def mirror_left(hidden, count, source_row, target_row):
    for pair in range(HALO // 2):
        first = hidden[pl.ds(at(HALO // 2, source_row + 2 * pair), count, stride=PITCH), :]
        second = hidden[pl.ds(at(HALO // 2, source_row + 2 * pair + 1), count, stride=PITCH), :]
        even, odd = swap_pixels(first, second)
        hidden[pl.ds(at(pair, target_row), count, stride=2), :] = even
        hidden[pl.ds(at(pair, target_row + 1), count, stride=2), :] = odd


def mirror_below(hidden):
    for pair in range(HALO // 2):
        source = (HALO + TILE) // 2 + pair
        first = hidden[pl.ds(at(source, HALO), TILE // 2, stride=2), :]
        second = hidden[pl.ds(at(source, HALO + 1), TILE // 2, stride=2), :]
        even, odd = swap_pixels(first, second)
        hidden[pl.ds(at(HALO // 2, HALO + TILE + 2 * pair), TILE // 2, stride=PITCH), :] = even
        hidden[pl.ds(at(HALO // 2, HALO + TILE + 2 * pair + 1), TILE // 2, stride=PITCH), :] = odd


def clear(hidden, pairs, first, last):
    for pair in pairs:
        hidden[pl.ds(at(pair, first), last - first), :] = jnp.zeros((last - first, LANES), F32)


def beyond_band(hidden, offset, bands):
    far = range((HALO + TILE) // 2, PAIRS)

    @pl.when(offset == bands - 2)
    def _():
        clear(hidden, far, 0, HALO)

    @pl.when(offset == bands - 1)
    def _():
        clear(hidden, range(HALO // 2, PAIRS), 0, HALO)
        clear(hidden, far, HALO, HALO + TILE)


def mirrored(hidden, offset):
    @pl.when(offset == 0)
    def _():
        mirror_left(hidden, (TILE + HALO) // 2, 0, HALO)
        mirror_below(hidden)

    @pl.when(offset == 1)
    def _():
        mirror_left(hidden, HALO // 2, TILE, TILE + HALO)


def conv_kernel(bands, rows, cols, conv, bias, out, state, hidden_a, hidden_b, weights):
    offset = lax.axis_index("off")
    for layer in range(LAYERS):
        layer_weights(conv, layer, weights.at[layer])
    bias_twice = jnp.concatenate([bias[...], bias[...]], axis=1)
    row_part = rows[...]
    for pair in range(PAIRS):
        value = row_part + cols[pair : pair + 1, :]
        state[pair] = value
        hidden_a[pl.ds(at(pair, 0), SIDE), :] = gelu(value)
    beyond_band(hidden_a, offset, bands)
    source, target = hidden_a, hidden_b
    for layer in range(LAYERS):
        conv_layer(layer, source, target, state, weights.at[layer], bias_twice[layer : layer + 1], out)
        if layer < LAYERS - 1:
            beyond_band(target, offset, bands)
            mirrored(target, offset)
        source, target = target, source


def conv_layer(layer, source, target, state, weights, bias, out):
    dilation = 2**layer
    first, last = ROWS[layer]
    height = last - first
    quads = quads_of(layer)
    step = quads[0][1] - quads[0][0]
    fit = 480 // height
    halves = [quads[0::2], quads[1::2]]
    rounds = -(-len(halves[0]) // fit)
    size = -(-len(halves[0]) // rounds)

    def body(*accs):
        accs = [accs[: 2 * size], accs[2 * size :]]

        def issue(turn):
            mine = [half[turn * size : (turn + 1) * size] for half in halves]
            for part in range(6):
                row_tap, side = divmod(part, 2)
                for mxu in range(2):
                    if mine[mxu]:
                        pltpu.matmul_push_rhs(weights[part], part % 2, mxu)
                for place in range(size):
                    for mxu in range(2):
                        if place >= len(mine[mxu]):
                            continue
                        left = mine[mxu][place][0] + (2 * side - 1) * step
                        row = first + (row_tap - 1) * dilation
                        lhs = jnp.concatenate(
                            [source[pl.ds(at(left + k * step, row), height), :] for k in range(2)], axis=1
                        ).astype(BF16)
                        acc = accs[mxu][(turn % 2) * size + place]
                        pltpu.matmul_acc_lhs(acc, lhs, part % 2 if place == 0 else None)

        def finish(turn):
            for place in range(size):
                for mxu in range(2):
                    mine = halves[mxu][turn * size : (turn + 1) * size]
                    if place >= len(mine):
                        continue
                    summed = pltpu.matmul_pop(accs[mxu][(turn % 2) * size + place])
                    for k, pair in enumerate(mine[place]):
                        value = state[pair, first:last] + (summed[:, k * LANES : (k + 1) * LANES] + bias)
                        if layer == LAYERS - 1:
                            column = (pair - HALO // 2) * LANES
                            out[0, 0, :, column : column + LANES] = value.astype(BF16)
                        else:
                            state[pair, first:last] = value
                            target[pl.ds(at(pair, first), height), :] = gelu(value)

        issue(0)
        for turn in range(1, rounds):
            issue(turn)
            finish(turn - 1)
        finish(rounds - 1)

    pl.run_scoped(body, *[pltpu.ACC(mxu)((height, 256), F32) for mxu in range(2) for _ in range(2 * size)])


def vmem(count):
    return [pl.BlockSpec(memory_space=pltpu.VMEM)] * count


def on_device(bands, bin_embed, block_slot, proj_weight, proj_bias, conv_weight, conv_bias):
    blocks = block_slot.shape[0]
    rows, cols = pl.pallas_call(
        gather_kernel,
        name="gather_bins",
        out_shape=[jax.ShapeDtypeStruct((SIDE, LANES), F32), jax.ShapeDtypeStruct((PAIRS, LANES), F32)],
        in_specs=[vmem(1)[0], pl.BlockSpec(memory_space=pltpu.SMEM), *vmem(2)],
        out_specs=vmem(2),
        scratch_shapes=[
            pltpu.VMEM((blocks, TILE // 2, LANES), BF16),
            pltpu.VMEM((SIDE, LANES), F32),
            pltpu.SemaphoreType.DMA((Z,)),
            pltpu.SemaphoreType.DMA((Z,)),
            pltpu.SemaphoreType.DMA((Z,)),
            pltpu.SemaphoreType.DMA((Z,)),
            pltpu.SemaphoreType.DMA((2 * Z,)),
            pltpu.SemaphoreType.DMA((2 * Z,)),
        ],
        compiler_params=pltpu.CompilerParams(collective_id=0, has_side_effects=True),
    )(bin_embed, block_slot, proj_weight, proj_bias.reshape(1, -1))
    return conv_tiles(bands, rows, cols, conv_weight, conv_bias)


def conv_tiles(bands, rows, cols, conv_weight, conv_bias):
    return pl.pallas_call(
        functools.partial(conv_kernel, bands),
        name="conv_tiles",
        out_shape=jax.ShapeDtypeStruct((1, 1, TILE, TILE * TILE), BF16),
        in_specs=vmem(4),
        out_specs=vmem(1)[0],
        scratch_shapes=[
            pltpu.VMEM((PAIRS, SIDE, LANES), F32),
            pltpu.VMEM((PAIRS * PITCH, LANES), F32),
            pltpu.VMEM((PAIRS * PITCH, LANES), F32),
            pltpu.VMEM((LAYERS, 6, 256, 256), BF16),
        ],
    )(rows, cols, conv_weight, conv_bias)


def solution(mesh):
    placed = (P("pos", None), P(), P(), P(), P(), P())
    return jax.shard_map(
        functools.partial(on_device, mesh.shape["off"]),
        mesh=mesh,
        in_specs=placed,
        out_specs=P("pos", "off", None, None),
        check_vma=False,
    )
```

```python
import functools

import jax
import jax.numpy as jnp
from jax import lax
from jax.experimental import pallas as pl
from jax.experimental.pallas import tpu as pltpu
from jax.sharding import PartitionSpec as P

TILE = 64
LAYERS = 4
HALO = 16
SIDE = TILE + 2 * HALO
END = HALO + TILE
PAD = 8
PITCH = SIDE + 2 * PAD
LANES = 128
MOST = 47
F32 = jnp.float32
BF16 = jnp.bfloat16

X_LO, Z, CORE = 2, 8, 2

OUTER = 0.7978845608028654
SCALE = (OUTER * 0.044715) ** (1 / 3)
INNER = OUTER / SCALE

ROWS = ((0, 96), (0, 96), (8, 88), (16, 80))
TURNS = ((5, 4, 3), (4, 4, 3), (4, 4, 2), (4, 3, 1))
SLOTS = (0, 2, 1, 3)
PARTS = 5


def low_half(shape):
    return lax.broadcasted_iota(jnp.int32, shape, 1) < LANES // 2


def swap(value):
    return pltpu.roll(value, LANES // 2, 1)


def halves(left, right):
    return jnp.where(low_half(left.shape), left, right)


def prepare_weights(conv, out):
    zero = jnp.zeros((TILE, TILE), BF16)
    blank = jnp.zeros((TILE, LANES), BF16)
    for layer in range(LAYERS):
        for row_tap in range(3):
            taps = [
                conv[layer, :, (3 * row_tap + j) * TILE : (3 * row_tap + j + 1) * TILE] * jnp.asarray(0.5, BF16)
                for j in range(3)
            ]
            pieces = {
                -1: jnp.concatenate([zero, taps[0]], axis=1),
                0: jnp.concatenate([taps[0], taps[1]], axis=1),
                1: jnp.concatenate([taps[1], taps[2]], axis=1),
                2: jnp.concatenate([taps[2], zero], axis=1),
            }
            for tile in range(3):
                part, side = divmod(3 * row_tap + tile, 2)
                for slot, column in enumerate(SLOTS):
                    piece = pieces.get(2 * tile - column, blank)
                    out[layer, part, slot * TILE : (slot + 1) * TILE, side * LANES : (side + 1) * LANES] = piece
        for slot in range(4):
            out[layer, PARTS - 1, slot * TILE : (slot + 1) * TILE, LANES:] = blank


def gather_kernel(
    embed_in,
    weight_in,
    conv_in,
    slots_in,
    bias_in,
    conv_bias_in,
    rows_out,
    cols_out,
    weights_out,
    bias_out,
    embed,
    weight,
    conv,
    slots,
    bias,
    conv_bias,
    bins,
    cols,
    local_sem,
    send_sem,
    recv_sem,
    twin_send,
    twin_recv,
):
    loads = [
        pltpu.make_async_copy(here, there, local_sem.at[k])
        for k, (here, there) in enumerate(
            (
                (embed_in, embed),
                (weight_in, weight),
                (conv_in, conv),
                (slots_in, slots),
                (bias_in, bias),
                (conv_bias_in, conv_bias),
            )
        )
    ]
    for load in loads:
        load.start()
    me = lax.axis_index("pos")
    offset = lax.axis_index("off")
    blocks = X_LO * Z * CORE
    x = me // (Z * CORE)
    z = (me // CORE) % Z
    core = me % CORE

    def index(across, along, core_):
        return (((x + across) % X_LO) * Z + (z + along) % Z) * CORE + core_

    order = [(across, along) for along in (4, 3, 5, 2, 6, 1, 7, 0) for across in (1, 0)][:-1]
    peers = [index(*step, core) for step in order]
    twin = index(0, 0, 1 - core)
    barrier = pltpu.get_barrier_semaphore()
    for peer in [*peers, twin]:
        pl.semaphore_signal(barrier, inc=1, device_id={"pos": peer}, device_id_type=pl.DeviceIdType.MESH)
    half = TILE // 2
    loads[0].wait()
    loads[1].wait()
    packed = [
        lax.dot_general(
            embed[part * half : (part + 1) * half],
            weight[...],
            (((1,), (1,)), ((), ())),
            preferred_element_type=F32,
        )
        for part in range(2)
    ]
    bins[me] = jnp.concatenate(packed, axis=1).astype(BF16)
    pl.semaphore_wait(barrier, len(peers) + 1)

    def send(block, peer, send_to, recv_from):
        copy = pltpu.make_async_remote_copy(
            src_ref=bins.at[block],
            dst_ref=bins.at[block],
            send_sem=send_to,
            recv_sem=recv_from,
            device_id={"pos": peer},
            device_id_type=pl.DeviceIdType.MESH,
        )
        copy.start()
        return copy

    direct = [send(me, peer, send_sem.at[k], recv_sem.at[k]) for k, peer in enumerate(peers)]
    passed = [send(me, twin, twin_send.at[len(order)], twin_recv.at[len(order)])]
    for load in loads[2:]:
        load.wait()
    prepare_weights(conv, weights_out)
    bias_out[0:LAYERS] = SCALE * jnp.concatenate([conv_bias[...], conv_bias[...]], axis=1)
    for k, (across, along) in enumerate(order):
        direct[k].wait_recv()
        block = index(across, Z - along, core)
        passed.append(send(block, twin, twin_send.at[k], twin_recv.at[k]))
    for copy in passed:
        copy.wait_recv()
    for copy in [*direct, *passed]:
        copy.wait_send()

    def spread(base, out):
        def block(shift):
            return bins[slots[(base + shift + blocks) % blocks]].astype(F32) * SCALE

        before, here, after = block(-1), block(0), block(1)
        tail, head = before[half - HALO :], after[:HALO]
        out[0:HALO] = halves(swap(tail), tail)
        out[HALO : HALO + half] = halves(here, swap(here))
        out[HALO + half : END] = halves(swap(here), here)
        out[END:SIDE] = halves(head, swap(head))

    spread(me, rows_out)
    spread(me + offset, cols)
    left = cols[pl.ds(1, MOST, stride=2), :]
    right = cols[pl.ds(2, MOST, stride=2), :]
    cols_out[0:MOST] = halves(left, right) + SCALE * jnp.concatenate([bias[...], bias[...]], axis=1)


def hide(value):
    return value + value * jnp.tanh(value * (INNER + value * value))


def at(tile, row):
    return tile * PITCH + PAD + row


def keep_band(value, first, left, right, inside, corner):
    def factor(limits):
        kinds = [limits(left), limits(right)]
        if kinds == [None, None] or inside is None:
            return None
        rows = [jnp.ones((1, LANES), F32) if kind is None else kind for kind in kinds]
        return rows[0] if kinds[0] is kinds[1] else halves(*rows)

    top = factor(lambda column: None if column < HALO else inside if column < END else corner)
    middle = factor(lambda column: None if column < END else inside)
    pieces = []
    for low, high, scale in ((0, HALO, top), (HALO, END, middle), (END, SIDE, None)):
        low, high = max(low, first) - first, min(high - first, value.shape[0])
        if low < high:
            piece = value[low:high]
            pieces.append(piece if scale is None else piece * scale)
    return jnp.concatenate(pieces, axis=0)


def turned(hidden, tiles, row):
    block = jnp.stack([hidden[pl.ds(at(tile, row), 8), :] for tile in tiles], axis=0)
    block = jnp.swapaxes(block, 0, 1)
    return [block[k] for k in range(8)]


def target_columns(d, shift):
    groups = (SIDE - 2 * d) // (2 * d)
    span = max(8, 2 * d)
    for start in range(d, SIDE - d, span):
        places = []
        for column in range(start, min(start + span, SIDE - d)):
            group, inner = divmod(column - d, 2 * d)
            if inner < d:
                places.append((group * d + inner, column, column - start, column - start + d))
        yield [start + shift + 8 * k for k in range(span // 8)], places


def source_bundles(d, shift):
    groups = (SIDE - 2 * d) // (2 * d)
    if d == 2:
        for inner in range(d):
            for first in range(0, groups, 8):
                count = min(8, groups - first)
                tiles = [min(first + k, groups - 1) * d + inner for k in range(8)]
                rows = d + 2 * d * first + inner + shift
                yield tiles, [(half, 0, count, rows + half * d, 2 * d) for half in range(2)]
        return
    step = 8 // d
    for first in range(0, groups, step):
        tiles = [min(first + k // d, groups - 1) * d + k % d for k in range(8)]
        runs = []
        for k in range(min(step, groups - first)):
            rows = d + 2 * d * (first + k) + shift
            runs += [(half, k * d, d, rows + half * d, 1) for half in range(2)]
        yield tiles, runs


def clip(run, low, high):
    half, place, count, row, stride = run
    skip = max(0, -((row - low) // stride))
    stop = min(count, -((row - high) // stride))
    return half, place + skip, stop - skip, row + skip * stride, stride


def mirror(hidden, d, columns, rows, shift, keep=None):
    for tiles, runs in source_bundles(d, shift):
        runs = [clip(run, *rows) for run in runs]
        runs = [run for run in runs if run[2] > 0]
        if not runs:
            continue
        for reads, places in target_columns(d, shift):
            places = [p for p in places if p[1] + d >= columns[0] and p[1] < columns[1]]
            if not places:
                continue
            lines = {}
            for k, row in enumerate(reads):
                if any(p[2] // 8 == k or (p[3] // 8 == k and p[1] + d < columns[1]) for p in places):
                    for n, line in enumerate(turned(hidden, tiles, row)):
                        lines[8 * k + n] = line
            for tile, column, one, two in places:
                straddles = column + d >= columns[1]
                values = {}
                for half, place, count, row, stride in runs:
                    if half not in values:
                        if straddles:
                            values[half] = lines[one] if half == 0 else swap(lines[one])
                        elif half == 0:
                            values[half] = halves(lines[one], swap(lines[two]))
                        else:
                            values[half] = halves(swap(lines[one]), lines[two])
                    value = values[half][place : place + count]
                    goal = pl.ds(at(tile, row), count, stride=stride) if stride > 1 else pl.ds(at(tile, row), count)
                    if straddles or keep is not None:
                        old = hidden[goal, :]
                        if straddles:
                            value = halves(value, old)
                        if keep is not None:
                            value = jnp.where(jnp.broadcast_to(keep, value.shape) > 0, old, value)
                    hidden[goal, :] = value


def weave(main, side):
    done = 0
    for k, unit in enumerate(main):
        unit()
        upto = len(side) * (k + 1) // len(main)
        for extra in side[done:upto]:
            extra()
        done = upto
    for extra in side[done:]:
        extra()


def conv_kernel(bands, rows, cols, weights, bias, out, *scratch):
    offset = lax.axis_index("off")

    @pl.when(offset == 0)
    def _():
        conv_layers(bands, offset, True, rows, cols, weights, bias, out, *scratch)

    @pl.when(offset > 0)
    def _():
        conv_layers(bands, offset, False, rows, cols, weights, bias, out, *scratch)


def conv_layers(bands, offset, diagonal, rows, cols, weights, bias, out, state_a, state_b, hidden_a, hidden_b):
    def flag(holds):
        return jnp.broadcast_to(holds.astype(F32), (1, LANES))

    if diagonal:
        inside = corner = None
    else:
        inside, corner = flag(offset < bands - 1), flag(offset < bands - 2)
    keep = flag(offset != 1)

    def start(tile):
        value = rows[...] + cols[tile : tile + 1, :]
        state_a[tile] = value
        hidden_a[pl.ds(at(tile, 0), SIDE), :] = keep_band(hide(value), 0, 2 * tile + 1, 2 * tile + 2, inside, corner)

    source, target = (state_a, hidden_a), (state_b, hidden_b)
    for layer in range(LAYERS):
        conv_layer(layer, diagonal, source, target, weights.at[layer], bias[layer : layer + 1], out, inside, corner, start)
        d = 2 ** (layer + 1)
        if layer == LAYERS - 1:
            break
        if diagonal:
            mirror(target[1], d, (d, HALO), (HALO, SIDE - d), 0)
            mirror(target[1], d, (HALO, END), (END, SIDE - d), 0)
        else:
            mirror(target[1], d, (d, HALO), (END, SIDE - d), TILE, keep)
        source, target = target, source


def rows_of(layer, diagonal, quad):
    first, last = ROWS[layer]
    k, i = quad
    d = 2**layer
    column = 2 * d + 4 * d * k + i
    if diagonal and column + 3 * d < HALO:
        last = min(last, HALO)
    elif diagonal and column + 3 * d < END:
        last = min(last, END)
    if (last - first) % 16:
        return ROWS[layer]
    return first, last


def conv_layer(layer, diagonal, source, target, weights, bias, out, inside, corner, start):
    state, hidden = source
    next_state, next_hidden = target
    d = 2**layer
    quads = [(k, i) for k in range((SIDE - 4 * d) // (4 * d)) for i in range(d)]
    spans = {quad: rows_of(layer, diagonal, quad) for quad in quads}
    turns, begin = [], 0
    for size in TURNS[layer]:
        turns.append(quads[begin : begin + 2 * size])
        begin += 2 * size
    kinds, places = [], {}
    for turn, members in enumerate(turns):
        used = []
        for place, quad in enumerate(members):
            kind = (place % 2, turn % 2, spans[quad][1] - spans[quad][0])
            count = used.count(kind)
            used.append(kind)
            places[turn, place] = (*kind, count)
    kinds = sorted(set(places.values()))

    def inputs(quad):
        k, i = quad
        return [(2 * k + step) * d + i for step in range(3)]

    def body(*accs):
        accs = dict(zip(kinds, accs))

        def push(part):
            for mxu in range(2):
                pltpu.matmul_push_rhs(weights[part], part % 2, mxu, transpose=True)

        def multiply(turn, part, place):
            quad = turns[turn][place]
            tiles = inputs(quad)
            first, last = spans[quad]
            pieces = []
            for step in (2 * part, min(2 * part + 1, 8)):
                row_tap, tile = divmod(step, 3)
                pieces.append(hidden[pl.ds(at(tiles[tile], first + (row_tap - 1) * d), last - first), :])
            lhs = jnp.concatenate(pieces, axis=1).astype(BF16)
            pltpu.matmul_acc_lhs(accs[places[turn, place]], lhs, part % 2 if place < 2 else None)

        def issue(turn):
            units = []
            for part in range(PARTS):
                units.append(functools.partial(push, part))
                units += [functools.partial(multiply, turn, part, place) for place in range(len(turns[turn]))]
            return units

        def sums(turn, place):
            quad = turns[turn][place]
            first, last = spans[quad]
            summed = pltpu.matmul_pop(accs[places[turn, place]])
            before, here, after = [state[tile, first:last] for tile in inputs(quad)]
            return [
                summed[:, :LANES] + (halves(swap(before), here) + bias),
                summed[:, LANES:] + (halves(here, swap(after)) + bias),
            ]

        def finish(turn, place):
            quad = turns[turn][place]
            k, i = quad
            first, last = spans[quad]
            for step, value in enumerate(sums(turn, place)):
                column = 2 * d + 4 * d * k + i + step * d
                tile = k * 2 * d + i + step * d
                next_state[tile, first:last] = value
                next_hidden[pl.ds(at(tile, first), last - first), :] = keep_band(
                    hide(value), first, column, column + 2 * d, inside, corner
                )

        def finish_out(turn, place):
            k, i = turns[turn][place]
            for step, (even, odd) in enumerate(zip(sums(turn, place), sums(turn, place + 1))):
                even, odd = even * (1 / SCALE), odd * (1 / SCALE)
                for far, value in enumerate((halves(even, swap(odd)), halves(swap(even), odd))):
                    column = 4 * d * k + i + step * d + far * 2 * d
                    out[0, 0, :, column * TILE : column * TILE + LANES] = value.astype(BF16)

        def ends(turn):
            if layer == LAYERS - 1:
                return [functools.partial(finish_out, turn, place) for place in range(0, len(turns[turn]), 2)]
            return [functools.partial(finish, turn, place) for place in range(len(turns[turn]))]

        ready = 0
        for turn in range(len(turns)):
            side = []
            if layer == 0:
                if turn == 0:
                    ready = inputs(turns[0][-1])[-1] + 1
                    for tile in range(ready):
                        start(tile)
                upto = inputs(turns[turn + 1][-1])[-1] + 1 if turn + 1 < len(turns) else ready
                side += [functools.partial(start, tile) for tile in range(ready, upto)]
                ready = upto
            if turn > 0:
                side += ends(turn - 1)
            weave(issue(turn), side)
        for unit in ends(len(turns) - 1):
            unit()

    pl.run_scoped(body, *[pltpu.ACC(mxu)((height, 256), F32) for mxu, _, height, _ in kinds])


def vmem(count):
    return [pl.BlockSpec(memory_space=pltpu.VMEM)] * count


def on_device(bands, bin_embed, block_slot, proj_weight, proj_bias, conv_weight, conv_bias):
    blocks = block_slot.shape[0]
    inputs = [bin_embed, proj_weight.T, jnp.swapaxes(conv_weight, 1, 2), block_slot, proj_bias.reshape(1, -1), conv_bias]
    ready = pl.pallas_call(
        gather_kernel,
        name="gather_bins",
        out_shape=[
            pltpu.VMEM((SIDE, LANES), F32),
            pltpu.VMEM((MOST + 1, LANES), F32),
            pltpu.VMEM((LAYERS, PARTS, 256, 256), BF16),
            pltpu.VMEM((8, LANES), F32),
        ],
        in_specs=[pl.BlockSpec(memory_space=pltpu.HBM)] * len(inputs),
        out_specs=vmem(4),
        scratch_shapes=[
            *[
                (pltpu.SMEM if value is block_slot else pltpu.VMEM)(value.shape, value.dtype)
                for value in inputs
            ],
            pltpu.VMEM((blocks, TILE // 2, LANES), BF16),
            pltpu.VMEM((SIDE, LANES), F32),
            pltpu.SemaphoreType.DMA((len(inputs),)),
            *[pltpu.SemaphoreType.DMA((blocks // CORE,))] * 4,
        ],
        compiler_params=pltpu.CompilerParams(collective_id=0, has_side_effects=True, vmem_limit_bytes=32 * 2**20),
    )(*[pltpu.with_memory_space_constraint(value, pltpu.HBM) for value in inputs])
    ready = [pltpu.with_memory_space_constraint(value, pltpu.VMEM) for value in ready]
    return pl.pallas_call(
        functools.partial(conv_kernel, bands),
        name="conv_tiles",
        out_shape=jax.ShapeDtypeStruct((1, 1, TILE, TILE * TILE), BF16),
        in_specs=vmem(4),
        out_specs=vmem(1)[0],
        scratch_shapes=[
            *[pltpu.VMEM((MOST, SIDE, LANES), F32)] * 2,
            *[pltpu.VMEM((MOST * PITCH, LANES), F32)] * 2,
        ],
        compiler_params=pltpu.CompilerParams(vmem_limit_bytes=32 * 2**20),
    )(*ready)


def solution(mesh):
    placed = (P("pos", None), P(), P(), P(), P(), P())
    return jax.shard_map(
        functools.partial(on_device, mesh.shape["off"]),
        mesh=mesh,
        in_specs=placed,
        out_specs=P("pos", "off", None, None),
        check_vma=False,
    )
```

```python
import functools

import jax
import jax.numpy as jnp
from jax import lax
from jax.experimental import pallas as pl
from jax.experimental.pallas import tpu as pltpu
from jax.sharding import PartitionSpec as P

TILE = 64
LAYERS = 4
HALO = 16
SIDE = TILE + 2 * HALO
END = HALO + TILE
PAD = 8
PITCH = SIDE + 2 * PAD
LANES = 128
MOST = 47
F32 = jnp.float32
BF16 = jnp.bfloat16

X_LO, Z, CORE = 2, 8, 2
NEAR = 4

OUTER = 0.7978845608028654
SCALE = (OUTER * 0.044715) ** (1 / 3)
INNER = OUTER / SCALE

ROWS = ((0, 96), (0, 96), (8, 88), (16, 80))
TURNS = ((4, 4, 4), (4, 4, 3), (5, 5), (4, 4))
SLOTS = (0, 2, 1, 3)
PARTS = 5


def low_half(shape):
    return lax.broadcasted_iota(jnp.int32, shape, 1) < LANES // 2


def swap(value):
    return pltpu.roll(value, LANES // 2, 1)


def halves(left, right):
    return jnp.where(low_half(left.shape), left, right)


def prepare_weights(conv, out):
    zero = jnp.zeros((TILE, TILE), BF16)
    blank = jnp.zeros((TILE, LANES), BF16)
    for layer in range(LAYERS):
        for row_tap in range(3):
            taps = [
                conv[layer, :, (3 * row_tap + j) * TILE : (3 * row_tap + j + 1) * TILE] * jnp.asarray(0.5, BF16)
                for j in range(3)
            ]
            pieces = {
                -1: jnp.concatenate([zero, taps[0]], axis=1),
                0: jnp.concatenate([taps[0], taps[1]], axis=1),
                1: jnp.concatenate([taps[1], taps[2]], axis=1),
                2: jnp.concatenate([taps[2], zero], axis=1),
            }
            for tile in range(3):
                part, side = divmod(3 * row_tap + tile, 2)
                for slot, column in enumerate(SLOTS):
                    piece = pieces.get(2 * tile - column, blank)
                    out[layer, part, slot * TILE : (slot + 1) * TILE, side * LANES : (side + 1) * LANES] = piece
        for slot in range(4):
            out[layer, PARTS - 1, slot * TILE : (slot + 1) * TILE, LANES:] = blank


def gather_kernel(
    embed_in,
    weight_in,
    conv_in,
    slots_in,
    bias_in,
    conv_bias_in,
    rows_out,
    cols_out,
    weights_out,
    bias_out,
    embed,
    weight,
    conv,
    slots,
    bias,
    conv_bias,
    bins,
    cols,
    local_sem,
    send_sem,
    recv_sem,
    twin_send,
    twin_recv,
    ready_sem,
    all_sem,
):
    loads = [
        pltpu.make_async_copy(here, there, local_sem.at[k])
        for k, (here, there) in enumerate(
            (
                (embed_in, embed),
                (weight_in, weight),
                (conv_in, conv),
                (slots_in, slots),
                (bias_in, bias),
                (conv_bias_in, conv_bias),
            )
        )
    ]
    for load in loads:
        load.start()
    me = lax.axis_index("pos")
    offset = lax.axis_index("off")
    blocks = X_LO * Z * CORE
    x = me // (Z * CORE)
    z = (me // CORE) % Z
    core = me % CORE
    twin = me + 1 - 2 * core
    near = z < NEAR

    def index(across, along):
        return (across * Z + along) * CORE + core

    def other(across):
        return (x + across) % X_LO

    def place(block):
        return block // CORE

    near_chips = [(across, along) for along in range(NEAR) for across in range(X_LO)]
    far_chips = [(across, along) for along in range(NEAR, Z) for across in range(X_LO)]
    partner = Z - 1 - z
    barrier = pltpu.get_barrier_semaphore()

    def greet(peer, semaphore):
        pl.semaphore_signal(semaphore, inc=1, device_id={"pos": peer}, device_id_type=pl.DeviceIdType.MESH)

    def copy(block, peer, sends, receives):
        return pltpu.make_async_remote_copy(
            src_ref=bins.at[block],
            dst_ref=bins.at[block],
            send_sem=sends,
            recv_sem=receives,
            device_id={"pos": peer},
            device_id_type=pl.DeviceIdType.MESH,
        )

    def to_peer(block, peer):
        return copy(block, peer, send_sem.at[place(peer)], recv_sem.at[place(block)])

    def to_twin(block):
        return copy(block, twin, twin_send.at[place(block)], twin_recv.at[place(block)])

    def project():
        half = TILE // 2
        loads[0].wait()
        loads[1].wait()
        packed = [
            lax.dot_general(
                embed[part * half : (part + 1) * half],
                weight[...],
                (((1,), (1,)), ((), ())),
                preferred_element_type=F32,
            )
            for part in range(2)
        ]
        bins[me] = jnp.concatenate(packed, axis=1).astype(BF16)

    def prepare():
        for load in loads[2:]:
            load.wait()
        prepare_weights(conv, weights_out)
        bias_out[0:LAYERS] = SCALE * jnp.concatenate([conv_bias[...], conv_bias[...]], axis=1)

    def chips_by_distance():
        flip = jnp.logical_or(z < NEAR // 2, z >= Z - NEAR // 2)
        return [(across, jnp.where(flip, Z - 1 - k, NEAR + k)) for k in range(Z - NEAR) for across in (x, 1 - x)]

    def each(chips, act):
        for across, along in chips:
            act(index(across, along))

    def others(chips, act):
        for across, along in chips:
            block = index(across, along)

            @pl.when(block != me)
            def _():
                act(block)

    def arrive(block):
        to_peer(block, me).wait_recv()

    greet(twin, barrier)

    @pl.when(near)
    def _():
        others(near_chips, lambda peer: greet(peer, barrier))
        each(far_chips, lambda peer: greet(peer, barrier))
        project()
        pl.semaphore_wait(barrier, len(near_chips))
        others(near_chips, lambda peer: to_peer(me, peer).start())
        to_twin(me).start()

    @pl.when(jnp.logical_not(near))
    def _():
        project()
        pl.semaphore_wait(barrier, len(near_chips) + 1)
        each(near_chips, lambda peer: to_peer(me, peer).start())
        each(near_chips, lambda peer: greet(peer, ready_sem))
        to_twin(me).start()

    prepare()

    def pass_on(block):
        arrive(block)
        to_twin(block).start()

    @pl.when(near)
    def _():
        others(near_chips, pass_on)
        pl.semaphore_wait(ready_sem, len(far_chips))
        greet(index(x, partner), all_sem)
        each(far_chips, lambda peer: to_peer(me, peer).start())
        each(chips_by_distance(), pass_on)

    @pl.when(jnp.logical_not(near))
    def _():
        pl.semaphore_wait(all_sem, 1)
        others(far_chips, lambda peer: to_peer(me, peer).start())
        each(near_chips, pass_on)
        others(far_chips, pass_on)

    for chip in range(blocks // CORE):
        to_twin(2 * chip + 1 - core).wait_recv()
    for chip in range(blocks // CORE):
        to_twin(2 * chip + core).wait_send()
    others(near_chips, lambda peer: to_peer(me, peer).wait_send())
    others(far_chips, lambda peer: to_peer(me, peer).wait_send())

    def spread(base, out):
        def block(shift):
            return bins[slots[(base + shift + blocks) % blocks]].astype(F32) * SCALE

        half = TILE // 2
        before, here, after = block(-1), block(0), block(1)
        tail, head = before[half - HALO :], after[:HALO]
        out[0:HALO] = halves(swap(tail), tail)
        out[HALO : HALO + half] = halves(here, swap(here))
        out[HALO + half : END] = halves(swap(here), here)
        out[END:SIDE] = halves(head, swap(head))

    spread(me, rows_out)
    spread(me + offset, cols)
    left = cols[pl.ds(1, MOST, stride=2), :]
    right = cols[pl.ds(2, MOST, stride=2), :]
    cols_out[0:MOST] = halves(left, right) + SCALE * jnp.concatenate([bias[...], bias[...]], axis=1)


def hide(value):
    return value + value * jnp.tanh(value * (INNER + value * value))


def at(tile, row):
    return tile * PITCH + PAD + row


def keep_band(value, first, left, right, inside, corner):
    def factor(limits):
        kinds = [limits(left), limits(right)]
        if kinds == [None, None] or inside is None:
            return None
        rows = [jnp.ones((1, LANES), F32) if kind is None else kind for kind in kinds]
        return rows[0] if kinds[0] is kinds[1] else halves(*rows)

    top = factor(lambda column: None if column < HALO else inside if column < END else corner)
    middle = factor(lambda column: None if column < END else inside)
    pieces = []
    for low, high, scale in ((0, HALO, top), (HALO, END, middle), (END, SIDE, None)):
        low, high = max(low, first) - first, min(high - first, value.shape[0])
        if low < high:
            piece = value[low:high]
            pieces.append(piece if scale is None else piece * scale)
    return jnp.concatenate(pieces, axis=0)


def turned(hidden, tiles, row):
    block = jnp.stack([hidden[pl.ds(at(tile, row), 8), :] for tile in tiles], axis=0)
    block = jnp.swapaxes(block, 0, 1)
    return [block[k] for k in range(8)]


def target_columns(d, shift):
    groups = (SIDE - 2 * d) // (2 * d)
    span = max(8, 2 * d)
    for start in range(d, SIDE - d, span):
        places = []
        for column in range(start, min(start + span, SIDE - d)):
            group, inner = divmod(column - d, 2 * d)
            if inner < d:
                places.append((group * d + inner, column, column - start, column - start + d))
        yield [start + shift + 8 * k for k in range(span // 8)], places


def source_bundles(d, shift):
    groups = (SIDE - 2 * d) // (2 * d)
    if d == 2:
        for inner in range(d):
            for first in range(0, groups, 8):
                count = min(8, groups - first)
                tiles = [min(first + k, groups - 1) * d + inner for k in range(8)]
                rows = d + 2 * d * first + inner + shift
                yield tiles, [(half, 0, count, rows + half * d, 2 * d) for half in range(2)]
        return
    step = 8 // d
    for first in range(0, groups, step):
        tiles = [min(first + k // d, groups - 1) * d + k % d for k in range(8)]
        runs = []
        for k in range(min(step, groups - first)):
            rows = d + 2 * d * (first + k) + shift
            runs += [(half, k * d, d, rows + half * d, 1) for half in range(2)]
        yield tiles, runs


def clip(run, low, high):
    half, place, count, row, stride = run
    skip = max(0, -((row - low) // stride))
    stop = min(count, -((row - high) // stride))
    return half, place + skip, stop - skip, row + skip * stride, stride


def mirror(hidden, d, columns, rows, shift, keep=None):
    for tiles, runs in source_bundles(d, shift):
        runs = [clip(run, *rows) for run in runs]
        runs = [run for run in runs if run[2] > 0]
        if not runs:
            continue
        for reads, places in target_columns(d, shift):
            places = [p for p in places if p[1] + d >= columns[0] and p[1] < columns[1]]
            if not places:
                continue
            lines = {}
            for k, row in enumerate(reads):
                if any(p[2] // 8 == k or (p[3] // 8 == k and p[1] + d < columns[1]) for p in places):
                    for n, line in enumerate(turned(hidden, tiles, row)):
                        lines[8 * k + n] = line
            for tile, column, one, two in places:
                straddles = column + d >= columns[1]
                values = {}
                for half, place, count, row, stride in runs:
                    if half not in values:
                        if straddles:
                            values[half] = lines[one] if half == 0 else swap(lines[one])
                        elif half == 0:
                            values[half] = halves(lines[one], swap(lines[two]))
                        else:
                            values[half] = halves(swap(lines[one]), lines[two])
                    value = values[half][place : place + count]
                    goal = pl.ds(at(tile, row), count, stride=stride) if stride > 1 else pl.ds(at(tile, row), count)
                    if straddles or keep is not None:
                        old = hidden[goal, :]
                        if straddles:
                            value = halves(value, old)
                        if keep is not None:
                            value = jnp.where(jnp.broadcast_to(keep, value.shape) > 0, old, value)
                    hidden[goal, :] = value


def weave(main, side):
    done = 0
    for k, unit in enumerate(main):
        unit()
        upto = len(side) * (k + 1) // len(main)
        for extra in side[done:upto]:
            extra()
        done = upto
    for extra in side[done:]:
        extra()


class Writer:
    def __init__(self, out, staged, sems):
        self.out, self.staged, self.sems = out, staged, sems
        self.waiting, self.started = [], []

    def put(self, pair, value):
        self.staged[:, pair * LANES : (pair + 1) * LANES] = value
        self.waiting.append(pair)

    def copy(self, pair):
        lanes = slice(pair * LANES, (pair + 1) * LANES)
        return pltpu.make_async_copy(self.staged.at[:, lanes], self.out.at[0, 0, :, lanes], self.sems.at[pair])

    def flush(self):
        for pair in self.waiting:
            self.copy(pair).start()
        self.started += self.waiting
        self.waiting = []

    def end(self):
        self.flush()
        for pair in self.started:
            self.copy(pair).wait()


def conv_kernel(bands, rows, cols, weights, bias, out, staged, sems, *scratch):
    offset = lax.axis_index("off")

    @pl.when(offset == 0)
    def _():
        conv_layers(bands, offset, True, rows, cols, weights, bias, Writer(out, staged, sems), *scratch)

    @pl.when(offset > 0)
    def _():
        conv_layers(bands, offset, False, rows, cols, weights, bias, Writer(out, staged, sems), *scratch)


def conv_layers(bands, offset, diagonal, rows, cols, weights, bias, out, state_a, state_b, hidden_a, hidden_b):
    def flag(holds):
        return jnp.broadcast_to(holds.astype(F32), (1, LANES))

    if diagonal:
        inside = corner = None
    else:
        inside, corner = flag(offset < bands - 1), flag(offset < bands - 2)
    keep = flag(offset != 1)

    def start(tile):
        value = rows[...] + cols[tile : tile + 1, :]
        state_a[tile] = value
        hidden_a[pl.ds(at(tile, 0), SIDE), :] = keep_band(hide(value), 0, 2 * tile + 1, 2 * tile + 2, inside, corner)

    source, target = (state_a, hidden_a), (state_b, hidden_b)
    for layer in range(LAYERS):
        conv_layer(layer, diagonal, source, target, weights.at[layer], bias[layer : layer + 1], out, inside, corner, start)
        d = 2 ** (layer + 1)
        if layer == LAYERS - 1:
            out.end()
            break
        if diagonal:
            mirror(target[1], d, (d, HALO), (HALO, SIDE - d), 0)
            mirror(target[1], d, (HALO, END), (END, SIDE - d), 0)
        else:
            mirror(target[1], d, (d, HALO), (END, SIDE - d), TILE, keep)
        source, target = target, source


def rows_of(layer, diagonal, quad):
    first, last = ROWS[layer]
    k, i = quad
    d = 2**layer
    column = 2 * d + 4 * d * k + i
    if diagonal and column + 3 * d < HALO:
        last = min(last, HALO)
    elif diagonal and column + 3 * d < END:
        last = min(last, END)
    if (last - first) % 16:
        return ROWS[layer]
    return first, last


def conv_layer(layer, diagonal, source, target, weights, bias, out, inside, corner, start):
    state, hidden = source
    next_state, next_hidden = target
    d = 2**layer
    quads = [(k, i) for k in range((SIDE - 4 * d) // (4 * d)) for i in range(d)]
    spans = {quad: rows_of(layer, diagonal, quad) for quad in quads}
    turns, begin = [], 0
    for size in TURNS[layer]:
        turns.append(quads[begin : begin + 2 * size])
        begin += 2 * size
    kinds, places = [], {}
    for turn, members in enumerate(turns):
        used = []
        for place, quad in enumerate(members):
            kind = (place % 2, turn % 2, spans[quad][1] - spans[quad][0])
            count = used.count(kind)
            used.append(kind)
            places[turn, place] = (*kind, count)
    kinds = sorted(set(places.values()))

    def inputs(quad):
        k, i = quad
        return [(2 * k + step) * d + i for step in range(3)]

    def body(*accs):
        accs = dict(zip(kinds, accs))

        def push(part):
            for mxu in range(2):
                pltpu.matmul_push_rhs(weights[part], part % 2, mxu, transpose=True)

        def multiply(turn, part, place):
            quad = turns[turn][place]
            tiles = inputs(quad)
            first, last = spans[quad]
            pieces = []
            for step in (2 * part, min(2 * part + 1, 8)):
                row_tap, tile = divmod(step, 3)
                pieces.append(hidden[pl.ds(at(tiles[tile], first + (row_tap - 1) * d), last - first), :])
            lhs = jnp.concatenate(pieces, axis=1).astype(BF16)
            pltpu.matmul_acc_lhs(accs[places[turn, place]], lhs, part % 2 if place < 2 else None)

        def issue(turn):
            units = []
            for part in range(PARTS):
                units.append(functools.partial(push, part))
                units += [functools.partial(multiply, turn, part, place) for place in range(len(turns[turn]))]
            return units

        def sums(turn, place):
            quad = turns[turn][place]
            first, last = spans[quad]
            summed = pltpu.matmul_pop(accs[places[turn, place]])
            before, here, after = [state[tile, first:last] for tile in inputs(quad)]
            return [
                summed[:, :LANES] + (halves(swap(before), here) + bias),
                summed[:, LANES:] + (halves(here, swap(after)) + bias),
            ]

        def finish(turn, place):
            quad = turns[turn][place]
            k, i = quad
            first, last = spans[quad]
            for step, value in enumerate(sums(turn, place)):
                column = 2 * d + 4 * d * k + i + step * d
                tile = k * 2 * d + i + step * d
                next_state[tile, first:last] = value
                next_hidden[pl.ds(at(tile, first), last - first), :] = keep_band(
                    hide(value), first, column, column + 2 * d, inside, corner
                )

        def finish_out(turn, place):
            k, i = turns[turn][place]
            out.flush()
            for step, (even, odd) in enumerate(zip(sums(turn, place), sums(turn, place + 1))):
                even, odd = even * (1 / SCALE), odd * (1 / SCALE)
                for far, value in enumerate((halves(even, swap(odd)), halves(swap(even), odd))):
                    column = 4 * d * k + i + step * d + far * 2 * d
                    out.put(column // 2, value.astype(BF16))

        def ends(turn):
            if layer == LAYERS - 1:
                return [functools.partial(finish_out, turn, place) for place in range(0, len(turns[turn]), 2)]
            return [functools.partial(finish, turn, place) for place in range(len(turns[turn]))]

        ready = 0
        for turn in range(len(turns)):
            side = []
            if layer == 0:
                if turn == 0:
                    ready = inputs(turns[0][-1])[-1] + 1
                    for tile in range(ready):
                        start(tile)
                upto = inputs(turns[turn + 1][-1])[-1] + 1 if turn + 1 < len(turns) else ready
                side += [functools.partial(start, tile) for tile in range(ready, upto)]
                ready = upto
            if turn > 0:
                side += ends(turn - 1)
            weave(issue(turn), side)
        for unit in ends(len(turns) - 1):
            unit()

    pl.run_scoped(body, *[pltpu.ACC(mxu)((height, 256), F32) for mxu, _, height, _ in kinds])


def vmem(count):
    return [pl.BlockSpec(memory_space=pltpu.VMEM)] * count


def on_device(bands, bin_embed, block_slot, proj_weight, proj_bias, conv_weight, conv_bias):
    blocks = block_slot.shape[0]
    inputs = [bin_embed, proj_weight.T, jnp.swapaxes(conv_weight, 1, 2), block_slot, proj_bias.reshape(1, -1), conv_bias]
    ready = pl.pallas_call(
        gather_kernel,
        name="gather_bins",
        out_shape=[
            pltpu.VMEM((SIDE, LANES), F32),
            pltpu.VMEM((MOST + 1, LANES), F32),
            pltpu.VMEM((LAYERS, PARTS, 256, 256), BF16),
            pltpu.VMEM((8, LANES), F32),
        ],
        in_specs=[pl.BlockSpec(memory_space=pltpu.HBM)] * len(inputs),
        out_specs=vmem(4),
        scratch_shapes=[
            *[
                (pltpu.SMEM if value is block_slot else pltpu.VMEM)(value.shape, value.dtype)
                for value in inputs
            ],
            pltpu.VMEM((blocks, TILE // 2, LANES), BF16),
            pltpu.VMEM((SIDE, LANES), F32),
            pltpu.SemaphoreType.DMA((len(inputs),)),
            *[pltpu.SemaphoreType.DMA((blocks // CORE,))] * 4,
            *[pltpu.SemaphoreType.REGULAR] * 2,
        ],
        compiler_params=pltpu.CompilerParams(collective_id=0, has_side_effects=True, vmem_limit_bytes=32 * 2**20),
    )(*[pltpu.with_memory_space_constraint(value, pltpu.HBM) for value in inputs])
    ready = [pltpu.with_memory_space_constraint(value, pltpu.VMEM) for value in ready]
    return pl.pallas_call(
        functools.partial(conv_kernel, bands),
        name="conv_tiles",
        out_shape=jax.ShapeDtypeStruct((1, 1, TILE, TILE * TILE), BF16),
        in_specs=vmem(4),
        out_specs=pl.BlockSpec(memory_space=pl.ANY),
        scratch_shapes=[
            pltpu.VMEM((TILE, TILE * TILE), BF16),
            pltpu.SemaphoreType.DMA((TILE // 2,)),
            *[pltpu.VMEM((MOST, SIDE, LANES), F32)] * 2,
            *[pltpu.VMEM((MOST * PITCH, LANES), F32)] * 2,
        ],
        compiler_params=pltpu.CompilerParams(vmem_limit_bytes=32 * 2**20),
    )(*ready)


def solution(mesh):
    placed = (P("pos", None), P(), P(), P(), P(), P())
    return jax.shard_map(
        functools.partial(on_device, mesh.shape["off"]),
        mesh=mesh,
        in_specs=placed,
        out_specs=P("pos", "off", None, None),
        check_vma=False,
    )
```

```python
import functools

import jax
import jax.numpy as jnp
from jax import lax
from jax.experimental import pallas as pl
from jax.experimental.pallas import tpu as pltpu
from jax.sharding import PartitionSpec as P

TILE = 64
LAYERS = 4
HALO = 16
SIDE = TILE + 2 * HALO
END = HALO + TILE
PAD = 8
PITCH = SIDE + 2 * PAD
LANES = 128
MOST = 47
F32 = jnp.float32
BF16 = jnp.bfloat16

X_LO, Z, CORE = 2, 8, 2
NEAR = 4

OUTER = 0.7978845608028654
SCALE = (OUTER * 0.044715) ** (1 / 3)
INNER = OUTER / SCALE

ROWS = ((0, 96), (0, 96), (8, 88), (16, 80))
TURNS = ((4, 4, 4), (4, 4, 3), (5, 5), (4, 4))
SLOTS = (0, 2, 1, 3)
PARTS = 5


def low_half(shape):
    return lax.broadcasted_iota(jnp.int32, shape, 1) < LANES // 2


def swap(value):
    return pltpu.roll(value, LANES // 2, 1)


def halves(left, right):
    return jnp.where(low_half(left.shape), left, right)


def prepare_weights(conv, out):
    zero = jnp.zeros((TILE, TILE), BF16)
    blank = jnp.zeros((TILE, LANES), BF16)
    for layer in range(LAYERS):
        for row_tap in range(3):
            taps = [
                conv[layer, :, (3 * row_tap + j) * TILE : (3 * row_tap + j + 1) * TILE] * jnp.asarray(0.5, BF16)
                for j in range(3)
            ]
            pieces = {
                -1: jnp.concatenate([zero, taps[0]], axis=1),
                0: jnp.concatenate([taps[0], taps[1]], axis=1),
                1: jnp.concatenate([taps[1], taps[2]], axis=1),
                2: jnp.concatenate([taps[2], zero], axis=1),
            }
            for tile in range(3):
                part, side = divmod(3 * row_tap + tile, 2)
                for slot, column in enumerate(SLOTS):
                    piece = pieces.get(2 * tile - column, blank)
                    out[layer, part, slot * TILE : (slot + 1) * TILE, side * LANES : (side + 1) * LANES] = piece
        for slot in range(4):
            out[layer, PARTS - 1, slot * TILE : (slot + 1) * TILE, LANES:] = blank


def gather_kernel(
    embed_in,
    weight_in,
    conv_in,
    slots_in,
    bias_in,
    conv_bias_in,
    rows_out,
    cols_out,
    weights_out,
    bias_out,
    embed,
    weight,
    conv,
    slots,
    bias,
    conv_bias,
    bins,
    cols,
    local_sem,
    send_sem,
    recv_sem,
    twin_send,
    twin_recv,
    ready_sem,
    all_sem,
):
    loads = [
        pltpu.make_async_copy(here, there, local_sem.at[k])
        for k, (here, there) in enumerate(
            (
                (embed_in, embed),
                (weight_in, weight),
                (conv_in, conv),
                (slots_in, slots),
                (bias_in, bias),
                (conv_bias_in, conv_bias),
            )
        )
    ]
    for load in loads:
        load.start()
    me = lax.axis_index("pos")
    offset = lax.axis_index("off")
    blocks = X_LO * Z * CORE
    x = me // (Z * CORE)
    z = (me // CORE) % Z
    core = me % CORE
    twin = me + 1 - 2 * core
    near = z < NEAR

    def index(across, along):
        return (across * Z + along) * CORE + core

    def other(across):
        return (x + across) % X_LO

    def place(block):
        return block // CORE

    near_chips = [(across, along) for along in range(NEAR) for across in range(X_LO)]
    far_chips = [(across, along) for along in (7, 6, 4, 5) for across in range(X_LO)]
    barrier = pltpu.get_barrier_semaphore()

    def greet(peer, semaphore):
        pl.semaphore_signal(semaphore, inc=1, device_id={"pos": peer}, device_id_type=pl.DeviceIdType.MESH)

    def copy(block, peer, sends, receives):
        return pltpu.make_async_remote_copy(
            src_ref=bins.at[block],
            dst_ref=bins.at[block],
            send_sem=sends,
            recv_sem=receives,
            device_id={"pos": peer},
            device_id_type=pl.DeviceIdType.MESH,
        )

    def to_peer(block, peer):
        return copy(block, peer, send_sem.at[place(peer)], recv_sem.at[place(block)])

    def to_twin(block):
        return copy(block, twin, twin_send.at[place(block)], twin_recv.at[place(block)])

    def project():
        half = TILE // 2
        loads[0].wait()
        loads[1].wait()
        packed = [
            lax.dot_general(
                embed[part * half : (part + 1) * half],
                weight[...],
                (((1,), (1,)), ((), ())),
                preferred_element_type=F32,
            )
            for part in range(2)
        ]
        bins[me] = jnp.concatenate(packed, axis=1).astype(BF16)

    def prepare():
        for load in loads[2:]:
            load.wait()
        prepare_weights(conv, weights_out)
        bias_out[0:LAYERS] = SCALE * jnp.concatenate([conv_bias[...], conv_bias[...]], axis=1)

    def chips_by_distance():
        flip = jnp.logical_or(z < NEAR // 2, z >= Z - NEAR // 2)
        return [(across, jnp.where(flip, Z - 1 - k, NEAR + k)) for k in range(Z - NEAR) for across in (x, 1 - x)]

    def each(chips, act):
        for across, along in chips:
            act(index(across, along))

    def others(chips, act):
        for across, along in chips:
            block = index(across, along)

            @pl.when(block != me)
            def _():
                act(block)

    def arrive(block):
        to_peer(block, me).wait_recv()

    greet(twin, barrier)

    @pl.when(near)
    def _():
        others(near_chips, lambda peer: greet(peer, barrier))
        each(far_chips, lambda peer: greet(peer, barrier))
        project()
        pl.semaphore_wait(barrier, len(near_chips))
        others(near_chips, lambda peer: to_peer(me, peer).start())
        to_twin(me).start()

    @pl.when(jnp.logical_not(near))
    def _():
        project()
        pl.semaphore_wait(barrier, len(near_chips) + 1)
        each(near_chips, lambda peer: to_peer(me, peer).start())
        each(near_chips, lambda peer: greet(peer, ready_sem))
        to_twin(me).start()

    prepare()

    def pass_on(block):
        arrive(block)
        to_twin(block).start()

    @pl.when(near)
    def _():
        others(near_chips, pass_on)
        pl.semaphore_wait(ready_sem, len(far_chips))

        @pl.when(z == 0)
        def _():
            each([(x, along) for along in range(NEAR + 2, Z)], lambda peer: greet(peer, all_sem))

        @pl.when(z == NEAR - 1)
        def _():
            each([(x, along) for along in range(NEAR, NEAR + 2)], lambda peer: greet(peer, all_sem))

        each(far_chips, lambda peer: to_peer(me, peer).start())
        each(chips_by_distance(), pass_on)

    @pl.when(jnp.logical_not(near))
    def _():
        pl.semaphore_wait(all_sem, 1)
        others(far_chips, lambda peer: to_peer(me, peer).start())
        others(far_chips, pass_on)
        each(near_chips, pass_on)

    for chip in range(blocks // CORE):
        to_twin(2 * chip + 1 - core).wait_recv()
    for chip in range(blocks // CORE):
        to_twin(2 * chip + core).wait_send()
    others(near_chips, lambda peer: to_peer(me, peer).wait_send())
    others(far_chips, lambda peer: to_peer(me, peer).wait_send())

    def spread(base, out):
        def block(shift):
            return bins[slots[(base + shift + blocks) % blocks]].astype(F32) * SCALE

        half = TILE // 2
        before, here, after = block(-1), block(0), block(1)
        tail, head = before[half - HALO :], after[:HALO]
        out[0:HALO] = halves(swap(tail), tail)
        out[HALO : HALO + half] = halves(here, swap(here))
        out[HALO + half : END] = halves(swap(here), here)
        out[END:SIDE] = halves(head, swap(head))

    spread(me, rows_out)
    spread(me + offset, cols)
    left = cols[pl.ds(1, MOST, stride=2), :]
    right = cols[pl.ds(2, MOST, stride=2), :]
    cols_out[0:MOST] = halves(left, right) + SCALE * jnp.concatenate([bias[...], bias[...]], axis=1)


def hide(value):
    return value + value * jnp.tanh(value * (INNER + value * value))


def at(tile, row):
    return tile * PITCH + PAD + row


def keep_band(value, first, left, right, inside, corner):
    def factor(limits):
        kinds = [limits(left), limits(right)]
        if kinds == [None, None] or inside is None:
            return None
        rows = [jnp.ones((1, LANES), F32) if kind is None else kind for kind in kinds]
        return rows[0] if kinds[0] is kinds[1] else halves(*rows)

    top = factor(lambda column: None if column < HALO else inside if column < END else corner)
    middle = factor(lambda column: None if column < END else inside)
    pieces = []
    for low, high, scale in ((0, HALO, top), (HALO, END, middle), (END, SIDE, None)):
        low, high = max(low, first) - first, min(high - first, value.shape[0])
        if low < high:
            piece = value[low:high]
            pieces.append(piece if scale is None else piece * scale)
    return jnp.concatenate(pieces, axis=0)


def turned(hidden, tiles, row):
    block = jnp.stack([hidden[pl.ds(at(tile, row), 8), :] for tile in tiles], axis=0)
    block = jnp.swapaxes(block, 0, 1)
    return [block[k] for k in range(8)]


def target_columns(d, shift):
    groups = (SIDE - 2 * d) // (2 * d)
    span = max(8, 2 * d)
    for start in range(d, SIDE - d, span):
        places = []
        for column in range(start, min(start + span, SIDE - d)):
            group, inner = divmod(column - d, 2 * d)
            if inner < d:
                places.append((group * d + inner, column, column - start, column - start + d))
        yield [start + shift + 8 * k for k in range(span // 8)], places


def source_bundles(d, shift):
    groups = (SIDE - 2 * d) // (2 * d)
    if d == 2:
        for inner in range(d):
            for first in range(0, groups, 8):
                count = min(8, groups - first)
                tiles = [min(first + k, groups - 1) * d + inner for k in range(8)]
                rows = d + 2 * d * first + inner + shift
                yield tiles, [(half, 0, count, rows + half * d, 2 * d) for half in range(2)]
        return
    step = 8 // d
    for first in range(0, groups, step):
        tiles = [min(first + k // d, groups - 1) * d + k % d for k in range(8)]
        runs = []
        for k in range(min(step, groups - first)):
            rows = d + 2 * d * (first + k) + shift
            runs += [(half, k * d, d, rows + half * d, 1) for half in range(2)]
        yield tiles, runs


def clip(run, low, high):
    half, place, count, row, stride = run
    skip = max(0, -((row - low) // stride))
    stop = min(count, -((row - high) // stride))
    return half, place + skip, stop - skip, row + skip * stride, stride


def mirror(hidden, d, columns, rows, shift, keep=None):
    for tiles, runs in source_bundles(d, shift):
        runs = [clip(run, *rows) for run in runs]
        runs = [run for run in runs if run[2] > 0]
        if not runs:
            continue
        for reads, places in target_columns(d, shift):
            places = [p for p in places if p[1] + d >= columns[0] and p[1] < columns[1]]
            if not places:
                continue
            lines = {}
            for k, row in enumerate(reads):
                if any(p[2] // 8 == k or (p[3] // 8 == k and p[1] + d < columns[1]) for p in places):
                    for n, line in enumerate(turned(hidden, tiles, row)):
                        lines[8 * k + n] = line
            for tile, column, one, two in places:
                straddles = column + d >= columns[1]
                values = {}
                for half, place, count, row, stride in runs:
                    if half not in values:
                        if straddles:
                            values[half] = lines[one] if half == 0 else swap(lines[one])
                        elif half == 0:
                            values[half] = halves(lines[one], swap(lines[two]))
                        else:
                            values[half] = halves(swap(lines[one]), lines[two])
                    value = values[half][place : place + count]
                    goal = pl.ds(at(tile, row), count, stride=stride) if stride > 1 else pl.ds(at(tile, row), count)
                    if straddles or keep is not None:
                        old = hidden[goal, :]
                        if straddles:
                            value = halves(value, old)
                        if keep is not None:
                            value = jnp.where(jnp.broadcast_to(keep, value.shape) > 0, old, value)
                    hidden[goal, :] = value


def weave(main, side):
    done = 0
    for k, unit in enumerate(main):
        unit()
        upto = len(side) * (k + 1) // len(main)
        for extra in side[done:upto]:
            extra()
        done = upto
    for extra in side[done:]:
        extra()


class Writer:
    def __init__(self, out, staged, sems):
        self.out, self.staged, self.sems = out, staged, sems
        self.waiting, self.started = [], []

    def put(self, pair, value):
        self.staged[:, pair * LANES : (pair + 1) * LANES] = value
        self.waiting.append(pair)

    def copy(self, pair):
        lanes = slice(pair * LANES, (pair + 1) * LANES)
        return pltpu.make_async_copy(self.staged.at[:, lanes], self.out.at[0, 0, :, lanes], self.sems.at[pair])

    def flush(self):
        for pair in self.waiting:
            self.copy(pair).start()
        self.started += self.waiting
        self.waiting = []

    def end(self):
        self.flush()
        for pair in self.started:
            self.copy(pair).wait()


def conv_kernel(bands, rows, cols, weights, bias, out, staged, sems, *scratch):
    offset = lax.axis_index("off")

    @pl.when(offset > 0)
    def _():
        conv_layers(bands, offset, False, rows, cols, weights, bias, Writer(out, staged, sems), *scratch)

    @pl.when(offset == 0)
    def _():
        conv_layers(bands, offset, True, rows, cols, weights, bias, Writer(out, staged, sems), *scratch)


def conv_layers(bands, offset, diagonal, rows, cols, weights, bias, out, state_a, state_b, hidden_a, hidden_b):
    def flag(holds):
        return jnp.broadcast_to(holds.astype(F32), (1, LANES))

    if diagonal:
        inside = corner = None
    else:
        inside, corner = flag(offset < bands - 1), flag(offset < bands - 2)
    keep = flag(offset != 1)

    def start(tile):
        value = rows[...] + cols[tile : tile + 1, :]
        state_a[tile] = value
        hidden_a[pl.ds(at(tile, 0), SIDE), :] = keep_band(hide(value), 0, 2 * tile + 1, 2 * tile + 2, inside, corner)

    source, target = (state_a, hidden_a), (state_b, hidden_b)
    for layer in range(LAYERS):
        conv_layer(layer, diagonal, source, target, weights.at[layer], bias[layer : layer + 1], out, inside, corner, start)
        d = 2 ** (layer + 1)
        if layer == LAYERS - 1:
            out.end()
            break
        if diagonal:
            mirror(target[1], d, (d, HALO), (HALO, SIDE - d), 0)
            mirror(target[1], d, (HALO, END), (END, SIDE - d), 0)
        else:
            mirror(target[1], d, (d, HALO), (END, SIDE - d), TILE, keep)
        source, target = target, source


def rows_of(layer, diagonal, quad):
    first, last = ROWS[layer]
    k, i = quad
    d = 2**layer
    column = 2 * d + 4 * d * k + i
    if diagonal and column + 3 * d < HALO:
        last = min(last, HALO)
    elif diagonal and column + 3 * d < END:
        last = min(last, END)
    if (last - first) % 16:
        return ROWS[layer]
    return first, last


def conv_layer(layer, diagonal, source, target, weights, bias, out, inside, corner, start):
    state, hidden = source
    next_state, next_hidden = target
    d = 2**layer
    quads = [(k, i) for k in range((SIDE - 4 * d) // (4 * d)) for i in range(d)]
    spans = {quad: rows_of(layer, diagonal, quad) for quad in quads}
    turns, begin = [], 0
    for size in TURNS[layer]:
        turns.append(quads[begin : begin + 2 * size])
        begin += 2 * size
    kinds, places = [], {}
    for turn, members in enumerate(turns):
        used = []
        for place, quad in enumerate(members):
            kind = (place % 2, turn % 2, spans[quad][1] - spans[quad][0])
            count = used.count(kind)
            used.append(kind)
            places[turn, place] = (*kind, count)
    kinds = sorted(set(places.values()))

    def inputs(quad):
        k, i = quad
        return [(2 * k + step) * d + i for step in range(3)]

    def body(*accs):
        accs = dict(zip(kinds, accs))

        def push(part):
            for mxu in range(2):
                pltpu.matmul_push_rhs(weights[part], part % 2, mxu, transpose=True)

        def multiply(turn, part, place):
            quad = turns[turn][place]
            tiles = inputs(quad)
            first, last = spans[quad]
            pieces = []
            for step in (2 * part, min(2 * part + 1, 8)):
                row_tap, tile = divmod(step, 3)
                pieces.append(hidden[pl.ds(at(tiles[tile], first + (row_tap - 1) * d), last - first), :])
            lhs = jnp.concatenate(pieces, axis=1).astype(BF16)
            pltpu.matmul_acc_lhs(accs[places[turn, place]], lhs, part % 2 if place < 2 else None)

        def issue(turn):
            units = []
            for part in range(PARTS):
                units.append(functools.partial(push, part))
                units += [functools.partial(multiply, turn, part, place) for place in range(len(turns[turn]))]
            return units

        def sums(turn, place):
            quad = turns[turn][place]
            first, last = spans[quad]
            summed = pltpu.matmul_pop(accs[places[turn, place]])
            before, here, after = [state[tile, first:last] for tile in inputs(quad)]
            return [
                summed[:, :LANES] + (halves(swap(before), here) + bias),
                summed[:, LANES:] + (halves(here, swap(after)) + bias),
            ]

        def finish(turn, place):
            quad = turns[turn][place]
            k, i = quad
            first, last = spans[quad]
            for step, value in enumerate(sums(turn, place)):
                column = 2 * d + 4 * d * k + i + step * d
                tile = k * 2 * d + i + step * d
                next_state[tile, first:last] = value
                next_hidden[pl.ds(at(tile, first), last - first), :] = keep_band(
                    hide(value), first, column, column + 2 * d, inside, corner
                )

        def finish_out(turn, place):
            k, i = turns[turn][place]
            out.flush()
            for step, (even, odd) in enumerate(zip(sums(turn, place), sums(turn, place + 1))):
                even, odd = even * (1 / SCALE), odd * (1 / SCALE)
                for far, value in enumerate((halves(even, swap(odd)), halves(swap(even), odd))):
                    column = 4 * d * k + i + step * d + far * 2 * d
                    out.put(column // 2, value.astype(BF16))

        def ends(turn):
            if layer == LAYERS - 1:
                return [functools.partial(finish_out, turn, place) for place in range(0, len(turns[turn]), 2)]
            return [functools.partial(finish, turn, place) for place in range(len(turns[turn]))]

        ready = 0
        for turn in range(len(turns)):
            side = []
            if layer == 0:
                if turn == 0:
                    ready = inputs(turns[0][-1])[-1] + 1
                    for tile in range(ready):
                        start(tile)
                upto = inputs(turns[turn + 1][-1])[-1] + 1 if turn + 1 < len(turns) else ready
                side += [functools.partial(start, tile) for tile in range(ready, upto)]
                ready = upto
            if turn > 0:
                side += ends(turn - 1)
            weave(issue(turn), side)
        for unit in ends(len(turns) - 1):
            unit()

    pl.run_scoped(body, *[pltpu.ACC(mxu)((height, 256), F32) for mxu, _, height, _ in kinds])


def vmem(count):
    return [pl.BlockSpec(memory_space=pltpu.VMEM)] * count


def on_device(bands, bin_embed, block_slot, proj_weight, proj_bias, conv_weight, conv_bias):
    blocks = block_slot.shape[0]
    inputs = [bin_embed, proj_weight.T, jnp.swapaxes(conv_weight, 1, 2), block_slot, proj_bias.reshape(1, -1), conv_bias]
    ready = pl.pallas_call(
        gather_kernel,
        name="gather_bins",
        out_shape=[
            pltpu.VMEM((SIDE, LANES), F32),
            pltpu.VMEM((MOST + 1, LANES), F32),
            pltpu.VMEM((LAYERS, PARTS, 256, 256), BF16),
            pltpu.VMEM((8, LANES), F32),
        ],
        in_specs=[pl.BlockSpec(memory_space=pltpu.HBM)] * len(inputs),
        out_specs=vmem(4),
        scratch_shapes=[
            *[
                (pltpu.SMEM if value is block_slot else pltpu.VMEM)(value.shape, value.dtype)
                for value in inputs
            ],
            pltpu.VMEM((blocks, TILE // 2, LANES), BF16),
            pltpu.VMEM((SIDE, LANES), F32),
            pltpu.SemaphoreType.DMA((len(inputs),)),
            *[pltpu.SemaphoreType.DMA((blocks // CORE,))] * 4,
            *[pltpu.SemaphoreType.REGULAR] * 2,
        ],
        compiler_params=pltpu.CompilerParams(collective_id=0, has_side_effects=True, vmem_limit_bytes=32 * 2**20),
    )(*[pltpu.with_memory_space_constraint(value, pltpu.HBM) for value in inputs])
    ready = [pltpu.with_memory_space_constraint(value, pltpu.VMEM) for value in ready]
    return pl.pallas_call(
        functools.partial(conv_kernel, bands),
        name="conv_tiles",
        out_shape=jax.ShapeDtypeStruct((1, 1, TILE, TILE * TILE), BF16),
        in_specs=vmem(4),
        out_specs=pl.BlockSpec(memory_space=pl.ANY),
        scratch_shapes=[
            pltpu.VMEM((TILE, TILE * TILE), BF16),
            pltpu.SemaphoreType.DMA((TILE // 2,)),
            *[pltpu.VMEM((MOST, SIDE, LANES), F32)] * 2,
            *[pltpu.VMEM((MOST * PITCH, LANES), F32)] * 2,
        ],
        compiler_params=pltpu.CompilerParams(vmem_limit_bytes=32 * 2**20),
    )(*ready)


def solution(mesh):
    placed = (P("pos", None), P(), P(), P(), P(), P())
    return jax.shard_map(
        functools.partial(on_device, mesh.shape["off"]),
        mesh=mesh,
        in_specs=placed,
        out_specs=P("pos", "off", None, None),
        check_vma=False,
    )
```

```python
import functools

import jax
import jax.numpy as jnp
from jax import lax
from jax.experimental import pallas as pl
from jax.experimental.pallas import tpu as pltpu
from jax.sharding import PartitionSpec as P

TILE = 64
LAYERS = 4
HALO = 16
SIDE = TILE + 2 * HALO
END = HALO + TILE
PAD = 8
PITCH = SIDE + 2 * PAD
LANES = 128
MOST = 47
F32 = jnp.float32
BF16 = jnp.bfloat16

X_LO, Z, CORE = 2, 8, 2
NEAR = 4

OUTER = 0.7978845608028654
SCALE = (OUTER * 0.044715) ** (1 / 3)
INNER = OUTER / SCALE

ROWS = ((0, 96), (0, 96), (8, 88), (16, 80))
TURNS = ((4, 4, 4), (4, 4, 3), (5, 5), (4, 4))
SLOTS = (0, 2, 1, 3)
PARTS = 5


def low_half(shape):
    return lax.broadcasted_iota(jnp.int32, shape, 1) < LANES // 2


def swap(value):
    return pltpu.roll(value, LANES // 2, 1)


def halves(left, right):
    return jnp.where(low_half(left.shape), left, right)


def prepare_weights(conv, bias, out):
    eye = lax.broadcasted_iota(jnp.int32, (TILE, TILE), 0) == lax.broadcasted_iota(jnp.int32, (TILE, TILE), 1)
    lane = lax.broadcasted_iota(jnp.int32, (TILE, LANES), 1)
    zero = jnp.zeros((TILE, TILE), BF16)
    blank = jnp.zeros((TILE, LANES), BF16)
    for layer in range(LAYERS):
        for row_tap in range(3):
            taps = [
                conv[layer, :, (3 * row_tap + j) * TILE : (3 * row_tap + j + 1) * TILE] * jnp.asarray(0.5, BF16)
                for j in range(3)
            ]
            pieces = {
                -1: jnp.concatenate([zero, taps[0]], axis=1),
                0: jnp.concatenate([taps[0], taps[1]], axis=1),
                1: jnp.concatenate([taps[1], taps[2]], axis=1),
                2: jnp.concatenate([taps[2], zero], axis=1),
            }
            for tile in range(3):
                part, side = divmod(3 * row_tap + tile, 2)
                for slot, column in enumerate(SLOTS):
                    piece = pieces.get(2 * tile - column, blank)
                    out[layer, part, slot * TILE : (slot + 1) * TILE, side * LANES : (side + 1) * LANES] = piece
        whole = SCALE * bias[layer : layer + 1, :]
        high = whole.astype(BF16).astype(F32)
        terms = [jnp.sum(jnp.where(eye, term, 0.0), axis=1, keepdims=True) for term in (high, whole - high)]
        shift = jnp.where(lane == 0, terms[0], jnp.where(lane == 1, terms[1], 0.0)).astype(BF16)
        for slot in range(4):
            out[layer, PARTS - 1, slot * TILE : (slot + 1) * TILE, LANES:] = shift


def gather_kernel(
    embed_in,
    weight_in,
    conv_in,
    slots_in,
    bias_in,
    conv_bias_in,
    rows_out,
    cols_out,
    weights_out,
    embed,
    weight,
    conv,
    slots,
    bias,
    conv_bias,
    bins,
    cols,
    local_sem,
    send_sem,
    recv_sem,
    twin_send,
    twin_recv,
    ready_sem,
    all_sem,
):
    loads = [
        pltpu.make_async_copy(here, there, local_sem.at[k])
        for k, (here, there) in enumerate(
            (
                (embed_in, embed),
                (weight_in, weight),
                (conv_in, conv),
                (slots_in, slots),
                (bias_in, bias),
                (conv_bias_in, conv_bias),
            )
        )
    ]
    for load in loads:
        load.start()
    me = lax.axis_index("pos")
    offset = lax.axis_index("off")
    blocks = X_LO * Z * CORE
    x = me // (Z * CORE)
    z = (me // CORE) % Z
    core = me % CORE
    twin = me + 1 - 2 * core
    near = z < NEAR

    def index(across, along):
        return (across * Z + along) * CORE + core

    def other(across):
        return (x + across) % X_LO

    def place(block):
        return block // CORE

    near_chips = [(across, along) for along in range(NEAR) for across in range(X_LO)]
    far_chips = [(across, along) for along in (7, 6, 4, 5) for across in range(X_LO)]
    barrier = pltpu.get_barrier_semaphore()

    def greet(peer, semaphore):
        pl.semaphore_signal(semaphore, inc=1, device_id={"pos": peer}, device_id_type=pl.DeviceIdType.MESH)

    def copy(block, peer, sends, receives):
        return pltpu.make_async_remote_copy(
            src_ref=bins.at[block],
            dst_ref=bins.at[block],
            send_sem=sends,
            recv_sem=receives,
            device_id={"pos": peer},
            device_id_type=pl.DeviceIdType.MESH,
        )

    def to_peer(block, peer):
        return copy(block, peer, send_sem.at[place(peer)], recv_sem.at[place(block)])

    def to_twin(block):
        return copy(block, twin, twin_send.at[place(block)], twin_recv.at[place(block)])

    def project():
        half = TILE // 2
        loads[0].wait()
        loads[1].wait()
        packed = [
            lax.dot_general(
                embed[part * half : (part + 1) * half],
                weight[...],
                (((1,), (1,)), ((), ())),
                preferred_element_type=F32,
            )
            for part in range(2)
        ]
        bins[me] = jnp.concatenate(packed, axis=1).astype(BF16)

    def prepare():
        for load in loads[2:]:
            load.wait()
        prepare_weights(conv, conv_bias, weights_out)

    def chips_by_distance():
        flip = jnp.logical_or(z < NEAR // 2, z >= Z - NEAR // 2)
        return [(across, jnp.where(flip, Z - 1 - k, NEAR + k)) for k in range(Z - NEAR) for across in (x, 1 - x)]

    def each(chips, act):
        for across, along in chips:
            act(index(across, along))

    def others(chips, act):
        for across, along in chips:
            block = index(across, along)

            @pl.when(block != me)
            def _():
                act(block)

    def arrive(block):
        to_peer(block, me).wait_recv()

    greet(twin, barrier)

    @pl.when(near)
    def _():
        others(near_chips, lambda peer: greet(peer, barrier))
        each(far_chips, lambda peer: greet(peer, barrier))
        project()
        pl.semaphore_wait(barrier, len(near_chips))
        others(near_chips, lambda peer: to_peer(me, peer).start())
        to_twin(me).start()

    @pl.when(jnp.logical_not(near))
    def _():
        project()
        pl.semaphore_wait(barrier, len(near_chips) + 1)
        each(near_chips, lambda peer: to_peer(me, peer).start())
        each(near_chips, lambda peer: greet(peer, ready_sem))
        to_twin(me).start()

    prepare()

    def pass_on(block):
        arrive(block)
        to_twin(block).start()

    @pl.when(near)
    def _():
        others(near_chips, pass_on)
        pl.semaphore_wait(ready_sem, len(far_chips))

        @pl.when(z == 0)
        def _():
            each([(x, along) for along in range(NEAR + 2, Z)], lambda peer: greet(peer, all_sem))

        @pl.when(z == NEAR - 1)
        def _():
            each([(x, along) for along in range(NEAR, NEAR + 2)], lambda peer: greet(peer, all_sem))

        each(far_chips, lambda peer: to_peer(me, peer).start())
        each(chips_by_distance(), pass_on)

    @pl.when(jnp.logical_not(near))
    def _():
        pl.semaphore_wait(all_sem, 1)
        others(far_chips, lambda peer: to_peer(me, peer).start())
        others(far_chips, pass_on)
        each(near_chips, pass_on)

    for chip in range(blocks // CORE):
        to_twin(2 * chip + 1 - core).wait_recv()
    for chip in range(blocks // CORE):
        to_twin(2 * chip + core).wait_send()
    others(near_chips, lambda peer: to_peer(me, peer).wait_send())
    others(far_chips, lambda peer: to_peer(me, peer).wait_send())

    def spread(base, out):
        def block(shift):
            return bins[slots[(base + shift + blocks) % blocks]].astype(F32) * SCALE

        half = TILE // 2
        before, here, after = block(-1), block(0), block(1)
        tail, head = before[half - HALO :], after[:HALO]
        out[0:HALO] = halves(swap(tail), tail)
        out[HALO : HALO + half] = halves(here, swap(here))
        out[HALO + half : END] = halves(swap(here), here)
        out[END:SIDE] = halves(head, swap(head))

    spread(me, rows_out)
    spread(me + offset, cols)
    left = cols[pl.ds(1, MOST, stride=2), :]
    right = cols[pl.ds(2, MOST, stride=2), :]
    cols_out[0:MOST] = halves(left, right) + SCALE * jnp.concatenate([bias[...], bias[...]], axis=1)


def hide(value):
    return value + value * jnp.tanh(value * (INNER + value * value))


def at(tile, row):
    return tile * PITCH + PAD + row


def keep_band(value, first, left, right, inside, corner):
    def factor(limits):
        kinds = [limits(left), limits(right)]
        if kinds == [None, None] or inside is None:
            return None
        rows = [jnp.ones((1, LANES), F32) if kind is None else kind for kind in kinds]
        return rows[0] if kinds[0] is kinds[1] else halves(*rows)

    top = factor(lambda column: None if column < HALO else inside if column < END else corner)
    middle = factor(lambda column: None if column < END else inside)
    pieces = []
    for low, high, scale in ((0, HALO, top), (HALO, END, middle), (END, SIDE, None)):
        low, high = max(low, first) - first, min(high - first, value.shape[0])
        if low < high:
            piece = value[low:high]
            pieces.append(piece if scale is None else piece * scale)
    return jnp.concatenate(pieces, axis=0)


def turned(hidden, tiles, row):
    block = jnp.stack([hidden[pl.ds(at(tile, row), 8), :] for tile in tiles], axis=0)
    block = jnp.swapaxes(block, 0, 1)
    return [block[k] for k in range(8)]


def target_columns(d, shift):
    groups = (SIDE - 2 * d) // (2 * d)
    span = max(8, 2 * d)
    for start in range(d, SIDE - d, span):
        places = []
        for column in range(start, min(start + span, SIDE - d)):
            group, inner = divmod(column - d, 2 * d)
            if inner < d:
                places.append((group * d + inner, column, column - start, column - start + d))
        yield [start + shift + 8 * k for k in range(span // 8)], places


def source_bundles(d, shift):
    groups = (SIDE - 2 * d) // (2 * d)
    if d == 2:
        for inner in range(d):
            for first in range(0, groups, 8):
                count = min(8, groups - first)
                tiles = [min(first + k, groups - 1) * d + inner for k in range(8)]
                rows = d + 2 * d * first + inner + shift
                yield tiles, [(half, 0, count, rows + half * d, 2 * d) for half in range(2)]
        return
    step = 8 // d
    for first in range(0, groups, step):
        tiles = [min(first + k // d, groups - 1) * d + k % d for k in range(8)]
        runs = []
        for k in range(min(step, groups - first)):
            rows = d + 2 * d * (first + k) + shift
            runs += [(half, k * d, d, rows + half * d, 1) for half in range(2)]
        yield tiles, runs


def clip(run, low, high):
    half, place, count, row, stride = run
    skip = max(0, -((row - low) // stride))
    stop = min(count, -((row - high) // stride))
    return half, place + skip, stop - skip, row + skip * stride, stride


def mirror(hidden, d, columns, rows, shift, keep=None):
    for tiles, runs in source_bundles(d, shift):
        runs = [clip(run, *rows) for run in runs]
        runs = [run for run in runs if run[2] > 0]
        if not runs:
            continue
        for reads, places in target_columns(d, shift):
            places = [p for p in places if p[1] + d >= columns[0] and p[1] < columns[1]]
            if not places:
                continue
            lines = {}
            for k, row in enumerate(reads):
                if any(p[2] // 8 == k or (p[3] // 8 == k and p[1] + d < columns[1]) for p in places):
                    for n, line in enumerate(turned(hidden, tiles, row)):
                        lines[8 * k + n] = line
            for tile, column, one, two in places:
                straddles = column + d >= columns[1]
                values = {}
                for half, place, count, row, stride in runs:
                    if half not in values:
                        if straddles:
                            values[half] = lines[one] if half == 0 else swap(lines[one])
                        elif half == 0:
                            values[half] = halves(lines[one], swap(lines[two]))
                        else:
                            values[half] = halves(swap(lines[one]), lines[two])
                    value = values[half][place : place + count]
                    goal = pl.ds(at(tile, row), count, stride=stride) if stride > 1 else pl.ds(at(tile, row), count)
                    if straddles or keep is not None:
                        old = hidden[goal, :]
                        if straddles:
                            value = halves(value, old)
                        if keep is not None:
                            value = jnp.where(jnp.broadcast_to(keep, value.shape) > 0, old, value)
                    hidden[goal, :] = value


def weave(main, side):
    done = 0
    for k, unit in enumerate(main):
        unit()
        upto = len(side) * (k + 1) // len(main)
        for extra in side[done:upto]:
            extra()
        done = upto
    for extra in side[done:]:
        extra()


class Writer:
    def __init__(self, out, staged, sems):
        self.out, self.staged, self.sems = out, staged, sems
        self.waiting, self.started = [], []

    def put(self, pair, value):
        self.staged[:, pair * LANES : (pair + 1) * LANES] = value
        self.waiting.append(pair)

    def copy(self, pair):
        lanes = slice(pair * LANES, (pair + 1) * LANES)
        return pltpu.make_async_copy(self.staged.at[:, lanes], self.out.at[0, 0, :, lanes], self.sems.at[pair])

    def flush(self):
        for pair in self.waiting:
            self.copy(pair).start()
        self.started += self.waiting
        self.waiting = []

    def end(self):
        self.flush()
        for pair in self.started:
            self.copy(pair).wait()


def conv_kernel(bands, rows, cols, weights, out, staged, sems, *scratch):
    offset = lax.axis_index("off")

    @pl.when(offset > 0)
    def _():
        conv_layers(bands, offset, False, rows, cols, weights, Writer(out, staged, sems), *scratch)

    @pl.when(offset == 0)
    def _():
        conv_layers(bands, offset, True, rows, cols, weights, Writer(out, staged, sems), *scratch)


def conv_layers(bands, offset, diagonal, rows, cols, weights, out, state_a, state_b, hidden_a, hidden_b):
    def flag(holds):
        return jnp.broadcast_to(holds.astype(F32), (1, LANES))

    if diagonal:
        inside = corner = None
    else:
        inside, corner = flag(offset < bands - 1), flag(offset < bands - 2)
    keep = flag(offset != 1)

    def start(tile):
        value = rows[...] + cols[tile : tile + 1, :]
        state_a[tile] = value
        hidden_a[pl.ds(at(tile, 0), SIDE), :] = keep_band(hide(value), 0, 2 * tile + 1, 2 * tile + 2, inside, corner)

    source, target = (state_a, hidden_a), (state_b, hidden_b)
    for layer in range(LAYERS):
        conv_layer(layer, diagonal, source, target, weights.at[layer], out, inside, corner, start)
        d = 2 ** (layer + 1)
        if layer == LAYERS - 1:
            out.end()
            break
        if diagonal:
            mirror(target[1], d, (d, HALO), (HALO, SIDE - d), 0)
            mirror(target[1], d, (HALO, END), (END, SIDE - d), 0)
        else:
            mirror(target[1], d, (d, HALO), (END, SIDE - d), TILE, keep)
        source, target = target, source


def rows_of(layer, diagonal, quad):
    first, last = ROWS[layer]
    k, i = quad
    d = 2**layer
    column = 2 * d + 4 * d * k + i
    if diagonal and column + 3 * d < HALO:
        last = min(last, HALO)
    elif diagonal and column + 3 * d < END:
        last = min(last, END)
    if (last - first) % 16:
        return ROWS[layer]
    return first, last


def conv_layer(layer, diagonal, source, target, weights, out, inside, corner, start):
    state, hidden = source
    next_state, next_hidden = target
    d = 2**layer
    quads = [(k, i) for k in range((SIDE - 4 * d) // (4 * d)) for i in range(d)]
    spans = {quad: rows_of(layer, diagonal, quad) for quad in quads}
    turns, begin = [], 0
    for size in TURNS[layer]:
        turns.append(quads[begin : begin + 2 * size])
        begin += 2 * size
    kinds, places = [], {}
    for turn, members in enumerate(turns):
        used = []
        for place, quad in enumerate(members):
            kind = (place % 2, turn % 2, spans[quad][1] - spans[quad][0])
            count = used.count(kind)
            used.append(kind)
            places[turn, place] = (*kind, count)
    kinds = sorted(set(places.values()))

    def inputs(quad):
        k, i = quad
        return [(2 * k + step) * d + i for step in range(3)]

    def body(*accs):
        accs = dict(zip(kinds, accs))

        def push(part):
            for mxu in range(2):
                pltpu.matmul_push_rhs(weights[part], part % 2, mxu, transpose=True)

        def multiply(turn, part, place):
            quad = turns[turn][place]
            tiles = inputs(quad)
            first, last = spans[quad]
            pieces = []
            for step in (2 * part, 2 * part + 1):
                row_tap, tile = divmod(step, 3)
                if row_tap == 3:
                    pieces.append(jnp.ones((last - first, LANES), BF16))
                    continue
                rows_in = pl.ds(at(tiles[tile], first + (row_tap - 1) * d), last - first)
                pieces.append(hidden[rows_in, :].astype(BF16))
            lhs = jnp.concatenate(pieces, axis=1)
            pltpu.matmul_acc_lhs(accs[places[turn, place]], lhs, part % 2 if place < 2 else None)

        def issue(turn):
            units = []
            for part in range(PARTS):
                units.append(functools.partial(push, part))
                units += [functools.partial(multiply, turn, part, place) for place in range(len(turns[turn]))]
            return units

        def sums(turn, place):
            quad = turns[turn][place]
            first, last = spans[quad]
            summed = pltpu.matmul_pop(accs[places[turn, place]])
            before, here, after = [state[tile, first:last] for tile in inputs(quad)]
            return [
                summed[:, :LANES] + halves(swap(before), here),
                summed[:, LANES:] + halves(here, swap(after)),
            ]

        def finish(turn, place):
            quad = turns[turn][place]
            k, i = quad
            first, last = spans[quad]
            for step, value in enumerate(sums(turn, place)):
                column = 2 * d + 4 * d * k + i + step * d
                tile = k * 2 * d + i + step * d
                next_state[tile, first:last] = value
                next_hidden[pl.ds(at(tile, first), last - first), :] = keep_band(
                    hide(value), first, column, column + 2 * d, inside, corner
                )

        def finish_out(turn, place):
            k, i = turns[turn][place]
            out.flush()
            for step, (even, odd) in enumerate(zip(sums(turn, place), sums(turn, place + 1))):
                even, odd = even * (1 / SCALE), odd * (1 / SCALE)
                for far, value in enumerate((halves(even, swap(odd)), halves(swap(even), odd))):
                    column = 4 * d * k + i + step * d + far * 2 * d
                    out.put(column // 2, value.astype(BF16))

        def ends(turn):
            if layer == LAYERS - 1:
                return [functools.partial(finish_out, turn, place) for place in range(0, len(turns[turn]), 2)]
            return [functools.partial(finish, turn, place) for place in range(len(turns[turn]))]

        ready = 0
        for turn in range(len(turns)):
            side = []
            if layer == 0:
                if turn == 0:
                    ready = inputs(turns[0][-1])[-1] + 1
                    for tile in range(ready):
                        start(tile)
                upto = inputs(turns[turn + 1][-1])[-1] + 1 if turn + 1 < len(turns) else ready
                side += [functools.partial(start, tile) for tile in range(ready, upto)]
                ready = upto
            if turn > 0:
                side += ends(turn - 1)
            weave(issue(turn), side)
        for unit in ends(len(turns) - 1):
            unit()

    pl.run_scoped(body, *[pltpu.ACC(mxu)((height, 256), F32) for mxu, _, height, _ in kinds])


def vmem(count):
    return [pl.BlockSpec(memory_space=pltpu.VMEM)] * count


def on_device(bands, bin_embed, block_slot, proj_weight, proj_bias, conv_weight, conv_bias):
    blocks = block_slot.shape[0]
    inputs = [bin_embed, proj_weight.T, jnp.swapaxes(conv_weight, 1, 2), block_slot, proj_bias.reshape(1, -1), conv_bias]
    ready = pl.pallas_call(
        gather_kernel,
        name="gather_bins",
        out_shape=[
            pltpu.VMEM((SIDE, LANES), F32),
            pltpu.VMEM((MOST + 1, LANES), F32),
            pltpu.VMEM((LAYERS, PARTS, 256, 256), BF16),
        ],
        in_specs=[pl.BlockSpec(memory_space=pltpu.HBM)] * len(inputs),
        out_specs=vmem(3),
        scratch_shapes=[
            *[
                (pltpu.SMEM if value is block_slot else pltpu.VMEM)(value.shape, value.dtype)
                for value in inputs
            ],
            pltpu.VMEM((blocks, TILE // 2, LANES), BF16),
            pltpu.VMEM((SIDE, LANES), F32),
            pltpu.SemaphoreType.DMA((len(inputs),)),
            *[pltpu.SemaphoreType.DMA((blocks // CORE,))] * 4,
            *[pltpu.SemaphoreType.REGULAR] * 2,
        ],
        compiler_params=pltpu.CompilerParams(collective_id=0, has_side_effects=True, vmem_limit_bytes=32 * 2**20),
    )(*[pltpu.with_memory_space_constraint(value, pltpu.HBM) for value in inputs])
    ready = [pltpu.with_memory_space_constraint(value, pltpu.VMEM) for value in ready]
    return pl.pallas_call(
        functools.partial(conv_kernel, bands),
        name="conv_tiles",
        out_shape=jax.ShapeDtypeStruct((1, 1, TILE, TILE * TILE), BF16),
        in_specs=vmem(3),
        out_specs=pl.BlockSpec(memory_space=pl.ANY),
        scratch_shapes=[
            pltpu.VMEM((TILE, TILE * TILE), BF16),
            pltpu.SemaphoreType.DMA((TILE // 2,)),
            *[pltpu.VMEM((MOST, SIDE, LANES), F32)] * 2,
            *[pltpu.VMEM((MOST * PITCH, LANES), F32)] * 2,
        ],
        compiler_params=pltpu.CompilerParams(vmem_limit_bytes=32 * 2**20),
    )(*ready)


def solution(mesh):
    placed = (P("pos", None), P(), P(), P(), P(), P())
    return jax.shard_map(
        functools.partial(on_device, mesh.shape["off"]),
        mesh=mesh,
        in_specs=placed,
        out_specs=P("pos", "off", None, None),
        check_vma=False,
    )
```

```python
import functools

import jax
import jax.numpy as jnp
from jax import lax
from jax.experimental import pallas as pl
from jax.experimental.pallas import tpu as pltpu
from jax.sharding import PartitionSpec as P

TILE = 64
LAYERS = 4
HALO = 16
SIDE = TILE + 2 * HALO
END = HALO + TILE
PAD = 8
PITCH = SIDE + 2 * PAD
LANES = 128
MOST = 47
F32 = jnp.float32
BF16 = jnp.bfloat16

X_LO, Z, CORE = 2, 8, 2
NEAR = 4

OUTER = 0.7978845608028654
SCALE = (OUTER * 0.044715) ** (1 / 3)
INNER = OUTER / SCALE

ROWS = ((0, 96), (0, 96), (8, 88), (16, 80))
TURNS = ((4, 4, 4), (4, 4, 3), (5, 5), (4, 4))
SLOTS = (0, 2, 1, 3)
PARTS = 5


def low_half(shape):
    return lax.broadcasted_iota(jnp.int32, shape, 1) < LANES // 2


def swap(value):
    return pltpu.roll(value, LANES // 2, 1)


def halves(left, right):
    return jnp.where(low_half(left.shape), left, right)


def prepare_weights(conv, bias, out):
    eye = lax.broadcasted_iota(jnp.int32, (TILE, TILE), 0) == lax.broadcasted_iota(jnp.int32, (TILE, TILE), 1)
    lane = lax.broadcasted_iota(jnp.int32, (TILE, LANES), 1)
    zero = jnp.zeros((TILE, TILE), BF16)
    blank = jnp.zeros((TILE, LANES), BF16)
    for layer in range(LAYERS):
        for row_tap in range(3):
            taps = [
                conv[layer, :, (3 * row_tap + j) * TILE : (3 * row_tap + j + 1) * TILE] * jnp.asarray(0.5, BF16)
                for j in range(3)
            ]
            pieces = {
                -1: jnp.concatenate([zero, taps[0]], axis=1),
                0: jnp.concatenate([taps[0], taps[1]], axis=1),
                1: jnp.concatenate([taps[1], taps[2]], axis=1),
                2: jnp.concatenate([taps[2], zero], axis=1),
            }
            for tile in range(3):
                part, side = divmod(3 * row_tap + tile, 2)
                for slot, column in enumerate(SLOTS):
                    piece = pieces.get(2 * tile - column, blank)
                    out[layer, part, slot * TILE : (slot + 1) * TILE, side * LANES : (side + 1) * LANES] = piece
        whole = SCALE * bias[layer : layer + 1, :]
        high = whole.astype(BF16).astype(F32)
        terms = [jnp.sum(jnp.where(eye, term, 0.0), axis=1, keepdims=True) for term in (high, whole - high)]
        shift = jnp.where(lane == 0, terms[0], jnp.where(lane == 1, terms[1], 0.0)).astype(BF16)
        for slot in range(4):
            out[layer, PARTS - 1, slot * TILE : (slot + 1) * TILE, LANES:] = shift


def gather_kernel(
    embed_in,
    weight_in,
    conv_in,
    slots_in,
    bias_in,
    conv_bias_in,
    rows_out,
    cols_out,
    weights_out,
    embed,
    weight,
    conv,
    slots,
    bias,
    conv_bias,
    bins,
    cols,
    local_sem,
    send_sem,
    recv_sem,
    twin_send,
    twin_recv,
    ready_sem,
    all_sem,
):
    loads = [
        pltpu.make_async_copy(here, there, local_sem.at[k])
        for k, (here, there) in enumerate(
            (
                (embed_in, embed),
                (weight_in, weight),
                (conv_in, conv),
                (slots_in, slots),
                (bias_in, bias),
                (conv_bias_in, conv_bias),
            )
        )
    ]
    for load in loads:
        load.start()
    me = lax.axis_index("pos")
    offset = lax.axis_index("off")
    blocks = X_LO * Z * CORE
    x = me // (Z * CORE)
    z = (me // CORE) % Z
    core = me % CORE
    twin = me + 1 - 2 * core
    near = z < NEAR

    def index(across, along):
        return (across * Z + along) * CORE + core

    def other(across):
        return (x + across) % X_LO

    def place(block):
        return block // CORE

    near_chips = [(across, along) for along in range(NEAR) for across in range(X_LO)]
    far_chips = [(across, along) for along in (7, 6, 4, 5) for across in range(X_LO)]
    barrier = pltpu.get_barrier_semaphore()

    def greet(peer, semaphore):
        pl.semaphore_signal(semaphore, inc=1, device_id={"pos": peer}, device_id_type=pl.DeviceIdType.MESH)

    def copy(block, peer, sends, receives):
        return pltpu.make_async_remote_copy(
            src_ref=bins.at[block],
            dst_ref=bins.at[block],
            send_sem=sends,
            recv_sem=receives,
            device_id={"pos": peer},
            device_id_type=pl.DeviceIdType.MESH,
        )

    def to_peer(block, peer):
        return copy(block, peer, send_sem.at[place(peer)], recv_sem.at[place(block)])

    def to_twin(block):
        return copy(block, twin, twin_send.at[place(block)], twin_recv.at[place(block)])

    def project():
        half = TILE // 2
        loads[0].wait()
        loads[1].wait()
        packed = [
            lax.dot_general(
                embed[part * half : (part + 1) * half],
                weight[...],
                (((1,), (1,)), ((), ())),
                preferred_element_type=F32,
            )
            for part in range(2)
        ]
        bins[me] = jnp.concatenate(packed, axis=1).astype(BF16)

    def prepare():
        for load in loads[2:]:
            load.wait()
        prepare_weights(conv, conv_bias, weights_out)

    def chips_by_distance():
        flip = jnp.logical_or(z < NEAR // 2, z >= Z - NEAR // 2)
        return [(across, jnp.where(flip, Z - 1 - k, NEAR + k)) for k in range(Z - NEAR) for across in (x, 1 - x)]

    def each(chips, act):
        for across, along in chips:
            act(index(across, along))

    def others(chips, act):
        for across, along in chips:
            block = index(across, along)

            @pl.when(block != me)
            def _():
                act(block)

    def arrive(block):
        to_peer(block, me).wait_recv()

    greet(twin, barrier)

    @pl.when(near)
    def _():
        others(near_chips, lambda peer: greet(peer, barrier))
        each(far_chips, lambda peer: greet(peer, barrier))
        project()
        pl.semaphore_wait(barrier, len(near_chips))
        others(near_chips, lambda peer: to_peer(me, peer).start())
        to_twin(me).start()

    @pl.when(jnp.logical_not(near))
    def _():
        project()
        pl.semaphore_wait(barrier, len(near_chips) + 1)
        each(near_chips, lambda peer: to_peer(me, peer).start())
        each(near_chips, lambda peer: greet(peer, ready_sem))
        to_twin(me).start()

    prepare()

    def pass_on(block):
        arrive(block)
        to_twin(block).start()

    @pl.when(near)
    def _():
        others(near_chips, pass_on)
        pl.semaphore_wait(ready_sem, len(far_chips))

        @pl.when(z == 0)
        def _():
            each([(x, along) for along in range(NEAR + 2, Z)], lambda peer: greet(peer, all_sem))

        @pl.when(z == NEAR - 1)
        def _():
            each([(x, along) for along in range(NEAR, NEAR + 2)], lambda peer: greet(peer, all_sem))

        each(far_chips, lambda peer: to_peer(me, peer).start())
        each(chips_by_distance(), pass_on)

    @pl.when(jnp.logical_not(near))
    def _():
        pl.semaphore_wait(all_sem, 1)
        others(far_chips, lambda peer: to_peer(me, peer).start())
        others(far_chips, pass_on)
        each(near_chips, pass_on)

    for chip in range(blocks // CORE):
        to_twin(2 * chip + 1 - core).wait_recv()

    def spread(base, out):
        def block(shift):
            return bins[slots[(base + shift + blocks) % blocks]].astype(F32) * SCALE

        half = TILE // 2
        before, here, after = block(-1), block(0), block(1)
        tail, head = before[half - HALO :], after[:HALO]
        out[0:HALO] = halves(swap(tail), tail)
        out[HALO : HALO + half] = halves(here, swap(here))
        out[HALO + half : END] = halves(swap(here), here)
        out[END:SIDE] = halves(head, swap(head))

    spread(me, rows_out)
    spread(me + offset, cols)
    left = cols[pl.ds(1, MOST, stride=2), :]
    right = cols[pl.ds(2, MOST, stride=2), :]
    cols_out[0:MOST] = halves(left, right) + SCALE * jnp.concatenate([bias[...], bias[...]], axis=1)
    for chip in range(blocks // CORE):
        to_twin(2 * chip + core).wait_send()
    others(near_chips, lambda peer: to_peer(me, peer).wait_send())
    others(far_chips, lambda peer: to_peer(me, peer).wait_send())


def hide(value):
    return value + value * jnp.tanh(value * (INNER + value * value))


def at(tile, row):
    return tile * PITCH + PAD + row


def keep_band(value, first, left, right, inside, corner):
    def factor(limits):
        kinds = [limits(left), limits(right)]
        if kinds == [None, None] or inside is None:
            return None
        rows = [jnp.ones((1, LANES), F32) if kind is None else kind for kind in kinds]
        return rows[0] if kinds[0] is kinds[1] else halves(*rows)

    top = factor(lambda column: None if column < HALO else inside if column < END else corner)
    middle = factor(lambda column: None if column < END else inside)
    pieces = []
    for low, high, scale in ((0, HALO, top), (HALO, END, middle), (END, SIDE, None)):
        low, high = max(low, first) - first, min(high - first, value.shape[0])
        if low < high:
            piece = value[low:high]
            pieces.append(piece if scale is None else piece * scale)
    return jnp.concatenate(pieces, axis=0)


def turned(hidden, tiles, row):
    block = jnp.stack([hidden[pl.ds(at(tile, row), 8), :] for tile in tiles], axis=0)
    block = jnp.swapaxes(block, 0, 1)
    return [block[k] for k in range(8)]


def target_columns(d, shift):
    groups = (SIDE - 2 * d) // (2 * d)
    span = max(8, 2 * d)
    for start in range(d, SIDE - d, span):
        places = []
        for column in range(start, min(start + span, SIDE - d)):
            group, inner = divmod(column - d, 2 * d)
            if inner < d:
                places.append((group * d + inner, column, column - start, column - start + d))
        yield [start + shift + 8 * k for k in range(span // 8)], places


def source_bundles(d, shift):
    groups = (SIDE - 2 * d) // (2 * d)
    if d == 2:
        for inner in range(d):
            for first in range(0, groups, 8):
                count = min(8, groups - first)
                tiles = [min(first + k, groups - 1) * d + inner for k in range(8)]
                rows = d + 2 * d * first + inner + shift
                yield tiles, [(half, 0, count, rows + half * d, 2 * d) for half in range(2)]
        return
    step = 8 // d
    for first in range(0, groups, step):
        tiles = [min(first + k // d, groups - 1) * d + k % d for k in range(8)]
        runs = []
        for k in range(min(step, groups - first)):
            rows = d + 2 * d * (first + k) + shift
            runs += [(half, k * d, d, rows + half * d, 1) for half in range(2)]
        yield tiles, runs


def clip(run, low, high):
    half, place, count, row, stride = run
    skip = max(0, -((row - low) // stride))
    stop = min(count, -((row - high) // stride))
    return half, place + skip, stop - skip, row + skip * stride, stride


def mirror(hidden, d, columns, rows, shift, keep=None):
    for tiles, runs in source_bundles(d, shift):
        runs = [clip(run, *rows) for run in runs]
        runs = [run for run in runs if run[2] > 0]
        if not runs:
            continue
        for reads, places in target_columns(d, shift):
            places = [p for p in places if p[1] + d >= columns[0] and p[1] < columns[1]]
            if not places:
                continue
            lines = {}
            for k, row in enumerate(reads):
                if any(p[2] // 8 == k or (p[3] // 8 == k and p[1] + d < columns[1]) for p in places):
                    for n, line in enumerate(turned(hidden, tiles, row)):
                        lines[8 * k + n] = line
            for tile, column, one, two in places:
                straddles = column + d >= columns[1]
                values = {}
                for half, place, count, row, stride in runs:
                    if half not in values:
                        if straddles:
                            values[half] = lines[one] if half == 0 else swap(lines[one])
                        elif half == 0:
                            values[half] = halves(lines[one], swap(lines[two]))
                        else:
                            values[half] = halves(swap(lines[one]), lines[two])
                    value = values[half][place : place + count]
                    goal = pl.ds(at(tile, row), count, stride=stride) if stride > 1 else pl.ds(at(tile, row), count)
                    if straddles or keep is not None:
                        old = hidden[goal, :]
                        if straddles:
                            value = halves(value, old)
                        if keep is not None:
                            value = jnp.where(jnp.broadcast_to(keep, value.shape) > 0, old, value)
                    hidden[goal, :] = value


def weave(main, side):
    done = 0
    for k, unit in enumerate(main):
        unit()
        upto = len(side) * (k + 1) // len(main)
        for extra in side[done:upto]:
            extra()
        done = upto
    for extra in side[done:]:
        extra()


class Writer:
    def __init__(self, out, staged, sems):
        self.out, self.staged, self.sems = out, staged, sems
        self.waiting, self.started = [], []

    def put(self, pair, value):
        self.staged[:, pair * LANES : (pair + 1) * LANES] = value
        self.waiting.append(pair)

    def copy(self, pair):
        lanes = slice(pair * LANES, (pair + 1) * LANES)
        return pltpu.make_async_copy(self.staged.at[:, lanes], self.out.at[0, 0, :, lanes], self.sems.at[pair])

    def flush(self):
        for pair in self.waiting:
            self.copy(pair).start()
        self.started += self.waiting
        self.waiting = []

    def end(self):
        self.flush()
        for pair in self.started:
            self.copy(pair).wait()


def conv_kernel(bands, rows, cols, weights, out, staged, sems, *scratch):
    offset = lax.axis_index("off")

    @pl.when(offset > 0)
    def _():
        conv_layers(bands, offset, False, rows, cols, weights, Writer(out, staged, sems), *scratch)

    @pl.when(offset == 0)
    def _():
        conv_layers(bands, offset, True, rows, cols, weights, Writer(out, staged, sems), *scratch)


def conv_layers(bands, offset, diagonal, rows, cols, weights, out, state_a, state_b, hidden_a, hidden_b):
    def flag(holds):
        return jnp.broadcast_to(holds.astype(F32), (1, LANES))

    if diagonal:
        inside = corner = None
    else:
        inside, corner = flag(offset < bands - 1), flag(offset < bands - 2)
    keep = flag(offset != 1)

    def start(tile):
        value = rows[...] + cols[tile : tile + 1, :]
        state_a[tile] = value
        hidden_a[pl.ds(at(tile, 0), SIDE), :] = keep_band(hide(value), 0, 2 * tile + 1, 2 * tile + 2, inside, corner)

    source, target = (state_a, hidden_a), (state_b, hidden_b)
    for layer in range(LAYERS):
        conv_layer(layer, diagonal, source, target, weights.at[layer], out, inside, corner, start)
        d = 2 ** (layer + 1)
        if layer == LAYERS - 1:
            out.end()
            break
        if diagonal:
            mirror(target[1], d, (d, HALO), (HALO, SIDE - d), 0)
            mirror(target[1], d, (HALO, END), (END, SIDE - d), 0)
        else:
            mirror(target[1], d, (d, HALO), (END, SIDE - d), TILE, keep)
        source, target = target, source


def rows_of(layer, diagonal, quad):
    first, last = ROWS[layer]
    k, i = quad
    d = 2**layer
    column = 2 * d + 4 * d * k + i
    if diagonal and column + 3 * d < HALO:
        last = min(last, HALO)
    elif diagonal and column + 3 * d < END:
        last = min(last, END)
    if (last - first) % 16:
        return ROWS[layer]
    return first, last


def conv_layer(layer, diagonal, source, target, weights, out, inside, corner, start):
    state, hidden = source
    next_state, next_hidden = target
    d = 2**layer
    quads = [(k, i) for k in range((SIDE - 4 * d) // (4 * d)) for i in range(d)]
    spans = {quad: rows_of(layer, diagonal, quad) for quad in quads}
    turns, begin = [], 0
    for size in TURNS[layer]:
        turns.append(quads[begin : begin + 2 * size])
        begin += 2 * size
    kinds, places = [], {}
    for turn, members in enumerate(turns):
        used = []
        for place, quad in enumerate(members):
            kind = (place % 2, turn % 2, spans[quad][1] - spans[quad][0])
            count = used.count(kind)
            used.append(kind)
            places[turn, place] = (*kind, count)
    kinds = sorted(set(places.values()))

    def inputs(quad):
        k, i = quad
        return [(2 * k + step) * d + i for step in range(3)]

    def body(*accs):
        accs = dict(zip(kinds, accs))

        def push(part):
            for mxu in range(2):
                pltpu.matmul_push_rhs(weights[part], part % 2, mxu, transpose=True)

        def multiply(turn, part, place):
            quad = turns[turn][place]
            tiles = inputs(quad)
            first, last = spans[quad]
            pieces = []
            for step in (2 * part, 2 * part + 1):
                row_tap, tile = divmod(step, 3)
                if row_tap == 3:
                    pieces.append(jnp.ones((last - first, LANES), BF16))
                    continue
                rows_in = pl.ds(at(tiles[tile], first + (row_tap - 1) * d), last - first)
                pieces.append(hidden[rows_in, :].astype(BF16))
            lhs = jnp.concatenate(pieces, axis=1)
            pltpu.matmul_acc_lhs(accs[places[turn, place]], lhs, part % 2 if place < 2 else None)

        def issue(turn):
            units = []
            for part in range(PARTS):
                units.append(functools.partial(push, part))
                units += [functools.partial(multiply, turn, part, place) for place in range(len(turns[turn]))]
            return units

        def sums(turn, place):
            quad = turns[turn][place]
            first, last = spans[quad]
            summed = pltpu.matmul_pop(accs[places[turn, place]])
            before, here, after = [state[tile, first:last] for tile in inputs(quad)]
            return [
                summed[:, :LANES] + halves(swap(before), here),
                summed[:, LANES:] + halves(here, swap(after)),
            ]

        def finish(turn, place):
            quad = turns[turn][place]
            k, i = quad
            first, last = spans[quad]
            for step, value in enumerate(sums(turn, place)):
                column = 2 * d + 4 * d * k + i + step * d
                tile = k * 2 * d + i + step * d
                next_state[tile, first:last] = value
                next_hidden[pl.ds(at(tile, first), last - first), :] = keep_band(
                    hide(value), first, column, column + 2 * d, inside, corner
                )

        def finish_out(turn, place):
            k, i = turns[turn][place]
            out.flush()
            for step, (even, odd) in enumerate(zip(sums(turn, place), sums(turn, place + 1))):
                even, odd = even * (1 / SCALE), odd * (1 / SCALE)
                for far, value in enumerate((halves(even, swap(odd)), halves(swap(even), odd))):
                    column = 4 * d * k + i + step * d + far * 2 * d
                    out.put(column // 2, value.astype(BF16))

        def ends(turn):
            if layer == LAYERS - 1:
                return [functools.partial(finish_out, turn, place) for place in range(0, len(turns[turn]), 2)]
            return [functools.partial(finish, turn, place) for place in range(len(turns[turn]))]

        ready = 0
        for turn in range(len(turns)):
            side = []
            if layer == 0:
                if turn == 0:
                    ready = inputs(turns[0][-1])[-1] + 1
                    for tile in range(ready):
                        start(tile)
                upto = inputs(turns[turn + 1][-1])[-1] + 1 if turn + 1 < len(turns) else ready
                side += [functools.partial(start, tile) for tile in range(ready, upto)]
                ready = upto
            if turn > 0:
                side += ends(turn - 1)
            weave(issue(turn), side)
        for unit in ends(len(turns) - 1):
            unit()

    pl.run_scoped(body, *[pltpu.ACC(mxu)((height, 256), F32) for mxu, _, height, _ in kinds])


def vmem(count):
    return [pl.BlockSpec(memory_space=pltpu.VMEM)] * count


def on_device(bands, bin_embed, block_slot, proj_weight, proj_bias, conv_weight, conv_bias):
    blocks = block_slot.shape[0]
    inputs = [bin_embed, proj_weight.T, jnp.swapaxes(conv_weight, 1, 2), block_slot, proj_bias.reshape(1, -1), conv_bias]
    ready = pl.pallas_call(
        gather_kernel,
        name="gather_bins",
        out_shape=[
            pltpu.VMEM((SIDE, LANES), F32),
            pltpu.VMEM((MOST + 1, LANES), F32),
            pltpu.VMEM((LAYERS, PARTS, 256, 256), BF16),
        ],
        in_specs=[pl.BlockSpec(memory_space=pltpu.HBM)] * len(inputs),
        out_specs=vmem(3),
        scratch_shapes=[
            *[
                (pltpu.SMEM if value is block_slot else pltpu.VMEM)(value.shape, value.dtype)
                for value in inputs
            ],
            pltpu.VMEM((blocks, TILE // 2, LANES), BF16),
            pltpu.VMEM((SIDE, LANES), F32),
            pltpu.SemaphoreType.DMA((len(inputs),)),
            *[pltpu.SemaphoreType.DMA((blocks // CORE,))] * 4,
            *[pltpu.SemaphoreType.REGULAR] * 2,
        ],
        compiler_params=pltpu.CompilerParams(collective_id=0, has_side_effects=True, vmem_limit_bytes=32 * 2**20),
    )(*[pltpu.with_memory_space_constraint(value, pltpu.HBM) for value in inputs])
    ready = [pltpu.with_memory_space_constraint(value, pltpu.VMEM) for value in ready]
    return pl.pallas_call(
        functools.partial(conv_kernel, bands),
        name="conv_tiles",
        out_shape=jax.ShapeDtypeStruct((1, 1, TILE, TILE * TILE), BF16),
        in_specs=vmem(3),
        out_specs=pl.BlockSpec(memory_space=pl.ANY),
        scratch_shapes=[
            pltpu.VMEM((TILE, TILE * TILE), BF16),
            pltpu.SemaphoreType.DMA((TILE // 2,)),
            *[pltpu.VMEM((MOST, SIDE, LANES), F32)] * 2,
            *[pltpu.VMEM((MOST * PITCH, LANES), F32)] * 2,
        ],
        compiler_params=pltpu.CompilerParams(vmem_limit_bytes=32 * 2**20),
    )(*ready)


def solution(mesh):
    placed = (P("pos", None), P(), P(), P(), P(), P())
    return jax.shard_map(
        functools.partial(on_device, mesh.shape["off"]),
        mesh=mesh,
        in_specs=placed,
        out_specs=P("pos", "off", None, None),
        check_vma=False,
    )
```
